512 devices in a mesh: scen: 64 (over x_hi, z, core), node: 8 (over x_lo, y).
Axes of the slice: x: 4 (x_hi: 2, x_lo: 2; x = x_hi * 2 + x_lo), y: 4, z: 16, core: 2. Of those that a mesh axis runs over, the one named last changes fastest.
Arguments:
- link_blocks: float32 [2048, 256, 512], P(('scen', 'node'))
- inverse_blocks: float32 [2048, 256, 256], P(('scen', 'node')), as said below
- block_rows: int32 [2048], P(('scen', 'node')), may hold values from 64 to 256, as said below
- node_of: int32 [2048], P(('scen', 'node')), may hold values from 0 to 15, as said below
- slot_count: int32 [512], P(('scen', 'node')), may hold values from 1 to 4, as said below
- node_diag: float32 [16, 512], P('node'), may hold values from 0.5 to 2
- first_link: float32 [16, 512, 512], P('node', None, 'scen'), may hold values from -0.09375 to 0.09375
- first_diag: float32 [512], P('scen'), may hold values from 0.5 to 2
Outputs:
- node_factor: float32 [16, 512, 512], P('node', 'scen')
- first_schur: float32 [512, 512], P('scen')
The draws below stay inside these ranges and needn't reach their ends.
Inputs may be any that keep to these rules, and one draw needn't show every extreme that they name: `inverse_blocks`: each block is symmetric and positive definite. `block_rows`: rows at or past this count are padding. `node_of`: every slot held by a device names a node of that device's group: with g the device's index along node, nodes g * 2 to g * 2 + 1. `slot_count`: slots of a device at or past its count are ignored.
All inputs are finite; a program needn't handle non-finite values.
Results may differ from the reference program's by a relative error of at most 0.0003.
Values sent between devices are 32-bit elements; how exact they have to be, the bound alone decides.
A program may use at most 64 MiB of HBM per device.

```python
import math
import jax
import jax.numpy as jnp
from jax import lax

BLOCK = 256
LINK = 512
FIRST = 512
SLOTS = 4
NODE_GRP = 2
NODES = 16
SCEN = 2048


def draw_link_blocks(key, part):
    key_noise = jax.random.fold_in(jax.random.fold_in(key, 11), 0)
    key_weight = jax.random.fold_in(jax.random.fold_in(key, 11), 2)
    key_coef = jax.random.fold_in(jax.random.fold_in(key, 11), 3)
    key_pair = jax.random.fold_in(jax.random.fold_in(key, 11), 4)
    group_count = NODES // NODE_GRP
    scen_devices = SCEN // (SLOTS * group_count)
    noise_scale = math.sqrt(NODE_GRP / (BLOCK * scen_devices))
    noise = jnp.clip(jax.random.normal(key_noise, (SCEN, BLOCK, LINK), jnp.float32), -4.0, 4.0)
    strengths = jnp.array([4.0, 8.0, 12.0, 16.0], jnp.float32)
    offset = jax.random.randint(key_pair, (), 0, scen_devices, dtype=jnp.int32)
    slot_place = jnp.arange(SCEN, dtype=jnp.int32) // SLOTS // group_count
    column_block = jnp.arange(LINK, dtype=jnp.int32) // (LINK // scen_devices)
    paired = (slot_place[:, None] + offset) % scen_devices == column_block[None, :]
    spike = jnp.where(paired, 2.5, 1.0).astype(jnp.float32)[:, None, :]
    column_weight = jax.random.normal(key_weight, (4, LINK), jnp.float32) * jnp.sqrt(strengths / LINK)[:, None]
    coef = jax.random.normal(key_coef, (SCEN, BLOCK, 4), jnp.float32) * (0.7 * noise_scale)
    common = coef[:, :, 0:1] * column_weight[0][None, None, :]
    common = common + coef[:, :, 1:2] * column_weight[1][None, None, :]
    common = common + coef[:, :, 2:3] * column_weight[2][None, None, :]
    common = common + coef[:, :, 3:4] * column_weight[3][None, None, :]
    return noise * spike * noise_scale + common


def draw_inverse_blocks(key, part):
    key_diag, key_noise = jax.random.split(key)
    diagonal = jax.random.uniform(key_diag, (SCEN, BLOCK), jnp.float32, 1.5, 3.0)
    raw_noise = jax.random.uniform(key_noise, (SCEN, BLOCK, BLOCK), jnp.float32, -1.0, 1.0) * (1.0 / math.sqrt(BLOCK))
    coupling = (raw_noise + jnp.swapaxes(raw_noise, 1, 2)) / 2.0
    return coupling + diagonal[:, :, None] * jnp.eye(BLOCK, dtype=jnp.float32)


def draw_block_rows(key, part):
    key_rows, key_long, key_short = jax.random.split(key, 3)
    row_counts = jax.random.randint(key_rows, (SCEN,), BLOCK // 4, BLOCK + 1, dtype=jnp.int32)
    long_slot = jax.random.randint(key_long, (), 0, SCEN, dtype=jnp.int32)
    short_slot = (long_slot + 1 + jax.random.randint(key_short, (), 0, SCEN - 1, dtype=jnp.int32)) % SCEN
    return row_counts.at[long_slot].set(BLOCK).at[short_slot].set(BLOCK // 4)


def draw_node_of(key, part):
    slot_ids = jnp.arange(SCEN, dtype=jnp.int32)
    node_group = slot_ids // SLOTS % (NODES // NODE_GRP)
    choose = jax.random.randint(key, (SCEN,), 0, NODE_GRP, dtype=jnp.int32)
    node_ids = node_group * NODE_GRP + choose
    return node_ids.at[0].set(0).at[SCEN - 1].set(NODES - 1)


def draw_slot_count(key, part):
    device_total = SCEN // SLOTS
    key_extra, key_busy, key_full, key_spare = jax.random.split(key, 4)
    extra_slots = jax.random.randint(key_extra, (device_total,), 0, SLOTS, dtype=jnp.int32)
    busy_device = jax.random.randint(key_busy, (device_total,), 0, 4, dtype=jnp.int32) == 0
    counts = 1 + jnp.where(busy_device, extra_slots, 0)
    full_device = jax.random.randint(key_full, (), 0, device_total, dtype=jnp.int32)
    spare_device = (full_device + 1 + jax.random.randint(key_spare, (), 0, device_total - 1, dtype=jnp.int32)) % device_total
    return counts.at[full_device].set(SLOTS).at[spare_device].set(1)


def level_of(stream_key, shape, cuts, least, high):
    def one(dim, shards_of):
        heights = jax.random.uniform(jax.random.fold_in(jax.random.fold_in(stream_key, 6), dim), (shards_of,), jnp.float32, least / len(cuts), high / len(cuts))
        return jnp.repeat(jnp.exp(heights), shape[dim] // shards_of).reshape((-1,) + (1,) * (len(shape) - dim - 1))

    factor_of = one(*cuts[0])
    for cut in cuts[1:]:
        factor_of = factor_of * one(*cut)
    return factor_of


def normal_values(rng, shape, scale, limit, cuts=(), kind=jnp.bfloat16):
    values = scale * jax.random.normal(rng, shape, jnp.float32)
    if cuts:
        values = values * level_of(rng, shape, cuts, -0.22, 0.18)
    return jnp.clip(values, -limit, limit).astype(kind)


def setup_inputs(seed: int = 0) -> dict:
    arg_keys = jax.random.split(jax.random.key(seed), 9)
    return {
        "link_blocks": draw_link_blocks(jax.random.fold_in(arg_keys[8], 71), 0),
        "inverse_blocks": draw_inverse_blocks(jax.random.fold_in(arg_keys[8], 71), 0),
        "block_rows": draw_block_rows(jax.random.fold_in(arg_keys[8], 71), 0),
        "node_of": draw_node_of(jax.random.fold_in(arg_keys[8], 71), 0),
        "slot_count": draw_slot_count(jax.random.fold_in(arg_keys[8], 71), 0),
        "node_diag": jnp.clip(jnp.exp(math.log(2.0) - 1.3862944 * jax.random.uniform(arg_keys[5], (NODES, LINK), jnp.float32) ** level_of(arg_keys[5], (NODES, LINK), ((0, 8),), -0.2, 0.2)), 0.5, 2.0),
        "first_link": normal_values(arg_keys[6], (NODES, LINK, FIRST), (LINK * NODES // 2) ** -0.5, 0.09375, ((0, 8), (2, 64)), jnp.float32),
        "first_diag": jnp.clip(jnp.exp(math.log(2.0) - 1.3862944 * jax.random.uniform(arg_keys[7], (FIRST,), jnp.float32) ** level_of(arg_keys[7], (FIRST,), ((0, 64),), -0.2, 0.2)), 0.5, 2.0),
    }


def slot_term(link_block, inverse_block, live_rows):
    row_ids = lax.broadcasted_iota(jnp.int32, (link_block.shape[0], 1), 0)
    masked = jnp.where(row_ids < live_rows, link_block, jnp.zeros_like(link_block))
    scaled = jnp.dot(inverse_block.astype(jnp.float32), masked.astype(jnp.float32), precision=lax.Precision.HIGHEST, preferred_element_type=jnp.float32)
    return lax.dot_general(masked.astype(jnp.float32), scaled.astype(jnp.float32), (((0,), (0,)), ((), ())), precision=lax.Precision.HIGHEST, preferred_element_type=jnp.float32)

def reference(link_blocks, inverse_blocks, block_rows, node_of, slot_count, node_diag, first_link, first_diag):
    slot_ids = jnp.arange(SCEN, dtype=jnp.int32)
    is_alive = slot_ids % SLOTS < slot_count[(slot_ids // SLOTS).astype(jnp.int32)]

    def add_slot(partial_value, slot_item):
        link_block, inverse_block, live_rows, node_id, alive_flag = slot_item
        contrib = slot_term(link_block, inverse_block, live_rows)
        contrib = jnp.where(alive_flag, contrib, jnp.zeros_like(contrib))
        node_index = node_id.astype(jnp.int32)
        current = lax.dynamic_index_in_dim(partial_value, node_index, 0, keepdims=False)
        return (lax.dynamic_update_index_in_dim(partial_value, current + contrib, node_index, 0), None)
    empty_sum = jnp.zeros((NODES, LINK, LINK), jnp.float32)
    schur_sum, _ = lax.scan(add_slot, empty_sum, (link_blocks, inverse_blocks, block_rows, node_of, is_alive))
    schur_sum = schur_sum + node_diag[:, :, None] * jnp.eye(LINK, dtype=jnp.float32)
    node_factor = jnp.linalg.cholesky(schur_sum)
    solved = lax.linalg.triangular_solve(node_factor, first_link, left_side=True, lower=True)
    first_schur = jnp.einsum('gwa,gwb->ab', solved, solved, precision=lax.Precision.HIGHEST) + jnp.diag(first_diag)
    return (node_factor, first_schur)
```

```python
import functools

import jax
import jax.numpy as jnp
from jax import lax
from jax.experimental import pallas as pl
from jax.experimental.pallas import tpu as pltpu
from jax.sharding import PartitionSpec as P

f32, bf16 = jnp.float32, jnp.bfloat16
NN = (((1,), (0,)), ((), ()))
NT = (((1,), (1,)), ((), ()))
TN = (((0,), (0,)), ((), ()))
Z = 16
K = 4
OFF = (0, 4, 7, 9)
TILES = 10
MESH = pl.DeviceIdType.MESH


def split(x):
    high = x.astype(bf16)
    return high, (x - high.astype(f32)).astype(bf16)


def mm(a, b, dims):
    def one(p, q):
        return lax.dot_general(p, q, dims, preferred_element_type=f32)

    return one(a[0], b[0]) + (one(a[0], b[1]) + one(a[1], b[0]))


def sub_row(x, k):
    return jnp.broadcast_to(x[k : k + 1, :], (8, 128))


def lane_col(x, j):
    return jnp.broadcast_to(x[:, j : j + 1], (8, 128))


def tree(terms):
    terms = list(terms)
    while len(terms) > 1:
        terms = [
            terms[i] + terms[i + 1] if i + 1 < len(terms) else terms[i]
            for i in range(0, len(terms), 2)
        ]
    return terms[0]


def eliminate(cols, sub):
    w = [jnp.zeros((8, 128), f32)] * 8
    n = list(cols)
    for i in range(8):
        hit = sub == i
        row = [sub_row(n[k], i) for k in range(8)]
        p = 1.0 / row[i]
        r = lax.rsqrt(row[i])
        m = jnp.where(hit, 0.0, n[i])
        for k in range(8):
            if k == i:
                continue
            c = row[k] * p
            if k < i:
                w[k] = jnp.where(hit, row[k] * r, w[k])
            n[k] = jnp.where(hit, c, n[k] - m * c)
        w[i] = jnp.where(hit, r, w[i])
        n[i] = jnp.where(hit, p, -m * p)
    return w, n


def diag_block(tiles):
    sub = lax.broadcasted_iota(jnp.int32, (8, 128), 0)
    lane = lax.broadcasted_iota(jnp.int32, (8, 128), 1)
    c = list(tiles)
    u, z = [None] * 16, [None] * 16
    e = [lane_col(c[0], k) for k in range(8)]
    for b in range(16):
        s = 8 * b
        here = (lane >= s) & (lane < s + 8)
        h = {t: [lane_col(c[t], s + m) for m in range(8)] for t in range(b + 1, 16)}
        if b < 15:
            old = [lane_col(c[b + 1], s + 8 + k) for k in range(8)]
        w, g = eliminate(e, sub)
        if b < 15:
            hn = h[b + 1]
            gc = [tree(sub_row(g[j], m) * hn[j] for j in range(8)) for m in range(8)]
            e = [
                old[k] - tree(hn[m] * sub_row(gc[m], k) for m in range(8))
                for k in range(8)
            ]
        own = c[b]
        aug = jnp.where(here, jnp.where(lane == s + sub, 1.0, 0.0), own)
        rows = [sub_row(own, k) for k in range(8)]
        rows_aug = [sub_row(aug, k) for k in range(8)]
        u[b] = jnp.where(
            lane >= s + sub, tree(w[k] * rows[k] for k in range(8)), 0.0
        )
        z[b] = jnp.where(lane < s + 8, tree(w[k] * rows_aug[k] for k in range(8)), 0.0)
        scaled = tree(g[k] * rows_aug[k] for k in range(8))
        spread = [sub_row(scaled, m) for m in range(8)]
        for t in range(b + 1, 16):
            c[t] = jnp.where(here, 0.0, c[t]) - tree(
                h[t][m] * spread[m] for m in range(8)
            )
    return jnp.concatenate(u, 0), jnp.concatenate(z, 0)


def place():
    s = lax.axis_index("scen")
    return s % 2, (s // 2) % Z, s // (2 * Z)


def scen_of(core, z, x):
    return {"scen": (x * Z + z) * 2 + core}


def remote(src, dst, send, recv, to):
    return pltpu.make_async_remote_copy(
        src_ref=src, dst_ref=dst, send_sem=send, recv_sem=recv,
        device_id=to, device_id_type=MESH,
    )


def sum_kernel(
    rows, nodes, count, link, inverse, diag, ft, s_out, f_out,
    acc, sib, mine, peer, rm, rp, one_s, one_r, ring_s, ring_r,
):
    core, z, x = place()
    group = lax.axis_index("node")
    down, up = scen_of(core, (z + Z - 1) % Z, x), scen_of(core, (z + 1) % Z, x)
    twin, across = scen_of(1 - core, z, x), scen_of(core, z, 1 - x)
    barrier = pltpu.get_barrier_semaphore()
    for to in (down, up, twin, across):
        pl.semaphore_signal(barrier, inc=1, device_id=to, device_id_type=MESH)
    pl.semaphore_wait(barrier, 4)

    sent = []

    def go(src, dst, send, recv, to):
        copy = remote(src, dst, send, recv, to)
        copy.start()
        sent.append(copy)
        return copy

    f_own = f_out.at[x, z, pl.ds(core * 8, 8), :]
    f_twin = go(ft.at[1 - core], f_own, one_s.at[0], one_r.at[0], twin)
    f_out[x, z, pl.ds(core * 8, 8), :] = ft[core]

    acc[...] = jnp.zeros_like(acc)
    row_id = lax.broadcasted_iota(jnp.int32, (link.shape[1], 1), 0)

    def slot(i, carry):
        limit = jnp.where(i < count[0], rows[i], 0)
        masked = jnp.where(row_id < limit, link[i], 0.0)
        first = nodes[i] == 2 * group
        m = split(masked)
        y = split(mm(split(inverse[i]), m, NN))
        for q in range(K):
            lo = 128 * q
            term = mm(
                (m[0][:, lo : lo + 128], m[1][:, lo : lo + 128]),
                (y[0][:, lo:], y[1][:, lo:]),
                TN,
            )
            for n in range(2):
                part = jnp.where(first, term, 0.0) if n == 0 else jnp.where(first, 0.0, term)
                for j in range(K - q):
                    acc[n, :, OFF[q] + j] += part[:, 128 * j : 128 * j + 128].reshape(
                        16, 8, 128
                    )
        return carry

    lax.fori_loop(0, link.shape[0], slot, 0)
    twin_sum = go(acc.at[1 - core], sib, one_s.at[1], one_r.at[1], twin)
    f_twin.wait_recv()
    f_across = go(f_out.at[x, z], f_out.at[x, z], one_s.at[2], one_r.at[2], across)
    twin_sum.wait_recv()
    acc[core] += sib[...]
    f_across.wait_recv()

    rs_m, rs_p, f_m, f_p = [], [], [], []
    for t in range(8):
        owner = (z + 8 + t) % Z
        if t == 0:
            src = acc.at[core, owner]
        else:
            rs_m[-1].wait_recv()
            rm[t - 1] += acc[core, owner]
            src = rm.at[t - 1]
        rs_m.append(go(src, rm.at[t], ring_s.at[0, t], ring_r.at[0, t], down))
        if t < 7:
            owner = (z + 7 - t) % Z
            if t == 0:
                src = acc.at[core, owner]
            else:
                rs_p[-1].wait_recv()
                rp[t - 1] += acc[core, owner]
                src = rp.at[t - 1]
            rs_p.append(go(src, rp.at[t], ring_s.at[1, t], ring_r.at[1, t], up))
        if t > 0:
            f_m[-1].wait_recv()
        piece = f_out.at[:, (z + t) % Z]
        f_m.append(go(piece, piece, ring_s.at[2, t], ring_r.at[2, t], down))
        if t < 7:
            if t > 0:
                f_p[-1].wait_recv()
            piece = f_out.at[:, (z + Z - t) % Z]
            f_p.append(go(piece, piece, ring_s.at[3, t], ring_r.at[3, t], up))
    rs_m[-1].wait_recv()
    rs_p[-1].wait_recv()
    mine[...] = acc[core, z] + (rm[7] + rp[6])
    swap = go(mine, peer, one_s.at[3], one_r.at[3], across)
    swap.wait_recv()
    sub = lax.broadcasted_iota(jnp.int32, (8, 128), 0)
    lane = lax.broadcasted_iota(jnp.int32, (8, 128), 1)
    s_out[z] = mine[...] + peer[...]
    for q in range(K):
        d = diag[:, 128 * q : 128 * q + 128]
        d = jnp.where(core == 0, d[0:1], d[1:2])
        s_out[z, OFF[q]] += jnp.where(lane == 8 * z + sub, jnp.broadcast_to(d, (8, 128)), 0.0)

    ag_m, ag_p = [], []
    for t in range(8):
        if t > 0:
            ag_m[-1].wait_recv()
        piece = s_out.at[(z + t) % Z]
        ag_m.append(go(piece, piece, ring_s.at[4, t], ring_r.at[4, t], down))
        if t < 7:
            if t > 0:
                ag_p[-1].wait_recv()
            piece = s_out.at[(z + Z - t) % Z]
            ag_p.append(go(piece, piece, ring_s.at[5, t], ring_r.at[5, t], up))
    for last in (ag_m, ag_p, f_m, f_p):
        last[-1].wait_recv()
    for copy in sent:
        copy.wait_send()


def factor_kernel(s_ref, f_ref, g_ref, l_ref, a, xt, low):
    core, z, x = place()
    own = pl.multiple_of((x * Z + z) * 16, 16)

    def block(i, j, q):
        if q == 0:
            return s_ref[:, OFF[i] + j - i].reshape(128, 128)
        return a[i, j]

    low[...] = jnp.zeros_like(low)
    for q in range(K):
        lo = 128 * q
        d = block(q, q, q)
        u, inv = diag_block([d[8 * t : 8 * t + 8, :] for t in range(16)])
        low[lo : lo + 128, lo : lo + 128] = u.T
        inv = split(inv)
        us = {}
        for j in range(q + 1, K):
            v = mm(inv, split(block(q, j, q)), NN)
            low[128 * j : 128 * j + 128, lo : lo + 128] = v.T
            us[j] = split(v)
        for i in range(q + 1, K):
            for j in range(i, K):
                a[i, j] = block(i, j, q) - mm(us[i], us[j], TN)
        src = f_ref if q == 0 else xt
        xq = mm(split(src[:, lo : lo + 128]), inv, NT)
        xt[:, lo : lo + 128] = xq
        xs = split(xq)
        for j in range(q + 1, K):
            hi = 128 * j
            xt[:, hi : hi + 128] = src[:, hi : hi + 128] - mm(xs, us[j], NN)
    g_ref[...] = mm(split(xt[pl.ds(own, 16), :]), split(xt[...]), NT).reshape(2, 8, -1)
    l_ref[...] = low[pl.ds(own, 16), :].reshape(2, 8, -1)


def share_kernel(groups, g_ref, l_ref, fd, l_out, first_out, got, send, recv, ls, lr):
    core, z, x = place()
    group = lax.axis_index("node")
    scen = lax.axis_index("scen")
    barrier = pltpu.get_barrier_semaphore()
    peers = []
    for c in range(2):
        for n in range(groups):
            if c == 0 and n == 0:
                continue
            to_core = (core + c) % 2
            to_node = (group + n) % groups
            peers.append(
                (to_core, to_node, {"scen": (x * Z + z) * 2 + to_core, "node": to_node})
            )
    for _, _, to in peers:
        pl.semaphore_signal(barrier, inc=1, device_id=to, device_id_type=MESH)
    pl.semaphore_wait(barrier, len(peers))
    copies = []
    for i, (to_core, _, to) in enumerate(peers):
        copies.append(
            remote(g_ref.at[to_core], got.at[core, group], send.at[i], recv.at[i], to)
        )
    twin = {"scen": (x * Z + z) * 2 + 1 - core}
    copies.append(remote(l_ref.at[1 - core], l_out.at[core], ls, lr, twin))
    for copy in copies:
        copy.start()
    l_out[core] = l_ref[core]
    got[core, group] = g_ref[core]
    for copy in copies:
        copy.wait()
    width = first_out.shape[1]
    sub = lax.broadcasted_iota(jnp.int32, (8, width), 0)
    lane = lax.broadcasted_iota(jnp.int32, (8, width), 1)
    total = tree(got[c, n] for c in range(2) for n in range(groups))
    first_out[...] = total + jnp.where(lane == scen * 8 + sub, fd[...], 0.0)


def shards(
    link_blocks, inverse_blocks, block_rows, node_of, slot_count, node_diag, first_link, first_diag
):
    groups = lax.axis_size("node")
    width = link_blocks.shape[2]
    ft = jnp.swapaxes(first_link, 1, 2)
    fd = jnp.broadcast_to(first_diag[:, None], (8, width))
    vmem = pl.BlockSpec(memory_space=pltpu.VMEM)
    smem = pl.BlockSpec(memory_space=pltpu.SMEM)
    dma = pltpu.SemaphoreType.DMA
    chunk = (TILES, 8, 128)
    s_all, f_all = pl.pallas_call(
        sum_kernel,
        out_shape=[
            jax.ShapeDtypeStruct((Z, *chunk), f32),
            jax.ShapeDtypeStruct((2, Z, 16, width), f32),
        ],
        in_specs=[smem] * 3 + [vmem] * 4,
        out_specs=[vmem] * 2,
        scratch_shapes=[
            pltpu.VMEM((2, Z, *chunk), f32),
            pltpu.VMEM((Z, *chunk), f32),
            pltpu.VMEM(chunk, f32),
            pltpu.VMEM(chunk, f32),
            pltpu.VMEM((8, *chunk), f32),
            pltpu.VMEM((7, *chunk), f32),
            dma((4,)),
            dma((4,)),
            dma((6, 8)),
            dma((6, 8)),
        ],
        compiler_params=pltpu.CompilerParams(
            collective_id=0, has_side_effects=True, vmem_limit_bytes=40 << 20
        ),
        name="sum_kernel",
    )(block_rows, node_of, slot_count, link_blocks, inverse_blocks, node_diag, ft)
    g_own, l_own = pl.pallas_call(
        factor_kernel,
        out_shape=[jax.ShapeDtypeStruct((2, 8, width), f32)] * 2,
        in_specs=[vmem] * 2,
        out_specs=[vmem] * 2,
        scratch_shapes=[
            pltpu.VMEM((K, K, 128, 128), f32),
            pltpu.VMEM((width, width), f32),
            pltpu.VMEM((width, width), f32),
        ],
        compiler_params=pltpu.CompilerParams(vmem_limit_bytes=40 << 20),
        name="factor_kernel",
    )(s_all, f_all.reshape(2 * Z * 16, width))
    node_factor, first_schur = pl.pallas_call(
        functools.partial(share_kernel, groups),
        out_shape=[
            jax.ShapeDtypeStruct((2, 8, width), f32),
            jax.ShapeDtypeStruct((8, width), f32),
        ],
        in_specs=[vmem] * 3,
        out_specs=[vmem] * 2,
        scratch_shapes=[
            pltpu.VMEM((2, groups, 8, width), f32),
            dma((2 * groups - 1,)),
            dma((2 * groups - 1,)),
            dma(()),
            dma(()),
        ],
        compiler_params=pltpu.CompilerParams(collective_id=1, has_side_effects=True),
        name="share_kernel",
    )(g_own, l_own, fd)
    return (node_factor, first_schur)


def solution(mesh):
    in_specs = (
        P(("scen", "node"), None, None),
        P(("scen", "node"), None, None),
        P(("scen", "node")),
        P(("scen", "node")),
        P(("scen", "node")),
        P("node", None),
        P("node", None, "scen"),
        P("scen"),
    )
    out_specs = (P("node", "scen", None), P("scen", None))
    return jax.shard_map(shards, mesh=mesh, in_specs=in_specs, out_specs=out_specs, check_vma=False)
```

```python
import functools

import jax
import jax.numpy as jnp
from jax import lax
from jax.experimental import pallas as pl
from jax.experimental.pallas import tpu as pltpu
from jax.sharding import PartitionSpec as P

f32, bf16 = jnp.float32, jnp.bfloat16
NN = (((1,), (0,)), ((), ()))
NT = (((1,), (1,)), ((), ()))
TN = (((0,), (0,)), ((), ()))
Z = 16
K = 4
WAVES = (
    ((0, 0),),
    ((0, 1), (0, 2), (0, 3)),
    ((1, 1), (1, 2), (1, 3)),
    ((2, 2), (2, 3), (3, 3)),
)
WAVE_OF = {block: (w, i) for w, wave in enumerate(WAVES) for i, block in enumerate(wave)}
FAR_FIRST = (8, 7, 9, 6, 10, 5, 11, 4, 12, 3, 13, 2, 14, 1, 15)
MESH = pl.DeviceIdType.MESH


def split(x):
    high = x.astype(bf16)
    return high, (x - high.astype(f32)).astype(bf16)


def mm(a, b, dims):
    def one(p, q):
        return lax.dot_general(p, q, dims, preferred_element_type=f32)

    return one(a[0], b[0]) + (one(a[0], b[1]) + one(a[1], b[0]))


def sub_row(x, k):
    return jnp.broadcast_to(x[k : k + 1, :], (8, 128))


def lane_col(x, j):
    return jnp.broadcast_to(x[:, j : j + 1], x.shape)


def stack(parts):
    return jnp.concatenate([x[None] for x in parts], 0)


def tree(terms):
    terms = list(terms)
    while len(terms) > 1:
        terms = [
            terms[i] + terms[i + 1] if i + 1 < len(terms) else terms[i]
            for i in range(0, len(terms), 2)
        ]
    return terms[0]


def eliminate(n, hit):
    w = None
    for i in range(8):
        row = jnp.broadcast_to(n[:, i : i + 1, :], (8, 8, 128))
        p = 1.0 / row[i]
        r = lax.rsqrt(row[i])
        m = jnp.where(hit[i], 0.0, n[i])
        c = row * p
        new = jnp.where(hit[i], c, n - m * c)
        parts = [new[:i]] if i else []
        parts.append(jnp.where(hit[i], p, -m * p)[None])
        if i < 7:
            parts.append(new[i + 1 :])
        n = jnp.concatenate(parts, 0)
        mine = jnp.where(hit[i], r, 0.0)[None]
        if i:
            mine = jnp.concatenate([jnp.where(hit[i], row[:i] * r, w), mine], 0)
        w = mine
    return w, n


def diag_block(c):
    sub = lax.broadcasted_iota(jnp.int32, (8, 128), 0)
    lane = lax.broadcasted_iota(jnp.int32, (8, 128), 1)
    hit = [sub == i for i in range(8)]
    u, z = [], []
    e = stack([lane_col(c[0:8], k) for k in range(8)])
    for b in range(16):
        s, rest = 8 * b, 120 - 8 * b
        here = (lane >= s) & (lane < s + 8)
        own = c[:8]
        if rest:
            c = c[8:]
            h = [lane_col(c, s + m) for m in range(8)]
            old = [lane_col(c[:8], s + 8 + k) for k in range(8)]
        w, g = eliminate(e, hit)
        if rest:
            hn = [x[:8] for x in h]
            gc = tree(jnp.broadcast_to(g[:, j : j + 1, :], (8, 8, 128)) * hn[j] for j in range(8))
            e = stack(
                [old[k] - tree(hn[m] * sub_row(gc[m], k) for m in range(8)) for k in range(8)]
            )
        aug = jnp.where(here, jnp.where(lane == s + sub, 1.0, 0.0), own)
        rows = [sub_row(aug, k) for k in range(8)]
        u.append(
            jnp.where(lane >= s + sub, tree(w[k] * sub_row(own, k) for k in range(8)), 0.0)
        )
        z.append(jnp.where(lane < s + 8, tree(w[k] * rows[k] for k in range(8)), 0.0))
        if rest:
            scaled = tree(g[k] * rows[k] for k in range(8))
            wide = lax.broadcasted_iota(jnp.int32, (rest, 128), 1)
            c = jnp.where((wide >= s) & (wide < s + 8), 0.0, c) - tree(
                h[m] * jnp.broadcast_to(scaled[m : m + 1], (rest, 128)) for m in range(8)
            )
    return jnp.concatenate(u, 0), jnp.concatenate(z, 0)


def remote(src, dst, send, recv, to):
    return pltpu.make_async_remote_copy(
        src_ref=src, dst_ref=dst, send_sem=send, recv_sem=recv,
        device_id=to, device_id_type=MESH,
    )


def kernel(
    groups, rows, nodes, count, fd, link_hbm, inverse_hbm, diag, ft, l_out, first_out,
    link, inverse, f_all, a, xt, low, g_own, got, load, one_s, one_r,
    f_s, f_r, f2_s, f2_r, end_s, end_r, *wave_refs,
):
    scen = lax.axis_index("scen")
    core, z, x = scen % 2, (scen // 2) % Z, scen // (2 * Z)
    group = lax.axis_index("node")

    def chip(dz):
        return {"scen": (x * Z + (z + dz) % Z) * 2 + core}

    twin = {"scen": scen + 1 - 2 * core}
    across = {"scen": ((1 - x) * Z + z) * 2 + core}
    finals = []
    for c in range(2):
        for n in range(groups):
            if c + n > 0:
                to_core = (core + c) % 2
                to = {"scen": scen - core + to_core, "node": (group + n) % groups}
                finals.append((to_core, to))
    barrier = pltpu.get_barrier_semaphore()
    greet = [chip(d) for d in range(1, Z)] + [across] + [to for _, to in finals]
    for to in greet:
        pl.semaphore_signal(barrier, inc=1, device_id=to, device_id_type=MESH)

    slots = link.shape[0]
    loads = []
    for i in range(slots):
        for n, (src, dst) in enumerate(((link_hbm, link), (inverse_hbm, inverse))):
            loads.append(pltpu.make_async_copy(src.at[i], dst.at[i], load.at[n, i]))
            loads[-1].start()

    waves = []
    per = len(wave_refs) // len(WAVES)
    for w in range(len(WAVES)):
        waves.append(wave_refs[per * w : per * w + per])
    sent = []

    def go(src, dst, send, recv, to):
        copy = remote(src, dst, send, recv, to)
        copy.start()
        sent.append(copy)
        return copy

    for acc, *_ in waves:
        acc[...] = jnp.zeros_like(acc)
    row_id = lax.broadcasted_iota(jnp.int32, (link.shape[1], 1), 0)
    for copy in loads:
        copy.wait()

    def slot(i, carry):
        limit = jnp.where(i < count[0], rows[i], 0)
        masked = jnp.where(row_id < limit, link[i], 0.0)
        first = nodes[i] == 2 * group
        m = split(masked)
        y = split(mm(split(inverse[i]), m, NN))
        for q in range(K):
            lo = 128 * q
            term = mm(
                (m[0][:, lo : lo + 128], m[1][:, lo : lo + 128]),
                (y[0][:, lo:], y[1][:, lo:]),
                TN,
            )
            for j in range(K - q):
                w, p = WAVE_OF[q, q + j]
                acc = waves[w][0]
                part = term[:, 128 * j : 128 * j + 128].reshape(16, 8, 128)
                acc[0, :, p] += jnp.where(first, part, 0.0)
                acc[1, :, p] += jnp.where(first, 0.0, part)
        return carry

    lax.fori_loop(0, slots, slot, 0)
    pl.semaphore_wait(barrier, len(greet))

    twins = []
    for w, (acc, sib, *_) in enumerate(waves):
        twins.append(go(acc.at[1 - core], sib, one_s.at[0, w], one_r.at[0, w], twin))
        if w == 0:
            f_own = f_all.at[x, z, pl.ds(core * 8, 8), :]
            f_twin = go(ft.at[1 - core], f_own, f_s.at[0], f_r.at[0], twin)
    f_all[x, z, pl.ds(core * 8, 8), :] = ft[core]

    parts = []
    for w, (acc, sib, rs, mine, peer, s_all, rs_s, rs_r, ag_s, ag_r) in enumerate(waves):
        twins[w].wait_recv()
        acc[core] += sib[...]
        parts.append(
            [
                go(acc.at[core, (z + d) % Z], rs.at[z], rs_s.at[d - 1], rs_r.at[d - 1], chip(d))
                for d in FAR_FIRST
            ]
        )
        rs[z] = acc[core, z]
        if w == 0:
            f_twin.wait_recv()
            f_across = go(f_all.at[x, z], f_all.at[x, z], f_s.at[1], f_r.at[1], across)

    f_across.wait_recv()
    piece = f_all.at[:, z]
    f_far = [
        go(piece, piece, f_s.at[2 + i], f_r.at[2 + i], chip(d)) for i, d in enumerate((8, 4, 12))
    ]

    def swap(w):
        acc, sib, rs, mine, peer, *_ = waves[w]
        for copy in parts[w]:
            copy.wait_recv()
        mine[...] = tree(rs[i] for i in range(Z))
        return go(mine, peer, one_s.at[1, w], one_r.at[1, w], across)

    sub = lax.broadcasted_iota(jnp.int32, (8, 128), 0)
    lane = lax.broadcasted_iota(jnp.int32, (8, 128), 1)

    def spread(w, swapped):
        acc, sib, rs, mine, peer, s_all, rs_s, rs_r, ag_s, ag_r = waves[w]
        swapped.wait_recv()
        s_all[z] = mine[...] + peer[...]
        for q in range(K):
            if WAVE_OF[q, q][0] == w:
                d = diag[:, 128 * q : 128 * q + 128]
                d = jnp.broadcast_to(jnp.where(core == 0, d[0:1], d[1:2]), (8, 128))
                s_all[z, WAVE_OF[q, q][1]] += jnp.where(lane == 8 * z + sub, d, 0.0)
        return [
            go(s_all.at[z], s_all.at[z], ag_s.at[d - 1], ag_r.at[d - 1], chip(d))
            for d in FAR_FIRST
        ]

    swap0 = swap(0)
    swap1 = swap(1)
    gather0 = spread(0, swap0)
    swap2 = swap(2)
    gather1 = spread(1, swap1)
    for copy in f_far:
        copy.wait_recv()
    f_near = []
    for i, d in enumerate((15, 1, 2)):
        for k in range(4):
            piece = f_all.at[:, (z + 4 * k) % Z]
            f_near.append(go(piece, piece, f2_s.at[i, k], f2_r.at[i, k], chip(d)))
    swap3 = swap(3)
    gather2 = spread(2, swap2)
    gather3 = spread(3, swap3)
    gathers = (gather0, gather1, gather2, gather3)

    def arrive(copies):
        for copy in copies:
            copy.wait_recv()

    def block(i, j):
        w, p = WAVE_OF[i, j]
        return waves[w][5][:, p].reshape(128, 128)

    low[...] = jnp.zeros_like(low)
    us, invs = {}, []

    def solve(q):
        lo = 128 * q
        src = xt
        if q == 0:
            part = f_all[...].reshape(4 * 128, -1)[:, lo : lo + 128]
        else:
            part = xt[:, lo : lo + 128]
        xq = mm(split(part), invs[q], NT)
        xs = split(xq)
        for j in range(q + 1, K):
            hi = 128 * j
            old = f_all[...].reshape(4 * 128, -1)[:, hi : hi + 128] if q == 0 else xt[:, hi : hi + 128]
            xt[:, hi : hi + 128] = old - mm(xs, us[q, j], NN)
        xt[:, lo : lo + 128] = xq

    arrive(gather0)
    for q in range(K):
        lo = 128 * q
        u, inv = diag_block(block(0, 0) if q == 0 else a[q, q])
        low[lo : lo + 128, lo : lo + 128] = u.T
        invs.append(split(inv))
        if q == 0:
            arrive(gather1)
        for j in range(q + 1, K):
            v = mm(invs[q], split(block(0, j) if q == 0 else a[q, j]), NN)
            low[128 * j : 128 * j + 128, lo : lo + 128] = v.T
            us[q, j] = split(v)
        if q == 0:
            arrive(gather2)
            for j in range(1, K):
                a[1, j] = block(1, j) - mm(us[0, 1], us[0, j], TN)
        elif q == 1:
            arrive(gather3)
            arrive(f_near)
            for i in range(2, K):
                for j in range(i, K):
                    a[i, j] = block(i, j) - (
                        mm(us[0, i], us[0, j], TN) + mm(us[1, i], us[1, j], TN)
                    )
            solve(0)
            solve(1)
        elif q == 2:
            a[3, 3] -= mm(us[2, 3], us[2, 3], TN)
            solve(2)
        else:
            solve(3)

    own = pl.multiple_of((x * Z + z) * 16, 16)
    width = first_out.shape[1]
    g_own[0] = low[pl.ds(own, 8), :]
    g_own[1] = low[pl.ds(pl.multiple_of(own + 8, 8), 8), :]
    factor = go(g_own.at[1 - core], l_out.at[core], end_s.at[0], end_r.at[0], twin)
    l_out[core] = g_own[core]
    term = mm(split(xt[pl.ds(own, 16), :]), split(xt[...]), NT)
    g_own[2] = term[:8]
    g_own[3] = term[8:]
    last = [
        go(g_own.at[2 + to_core], got.at[core, group], end_s.at[1 + i], end_r.at[1 + i], to)
        for i, (to_core, to) in enumerate(finals)
    ]
    got[core, group] = g_own[2 + core]
    arrive(last)
    row8 = lax.broadcasted_iota(jnp.int32, (8, width), 0)
    col8 = lax.broadcasted_iota(jnp.int32, (8, width), 1)
    d = jnp.zeros((8, width), f32)
    for i in range(8):
        d = jnp.where(row8 == i, fd[i], d)
    total = tree(got[c, n] for c in range(2) for n in range(groups))
    first_out[...] = total + jnp.where(col8 == scen * 8 + row8, d, 0.0)
    factor.wait_recv()
    for copy in sent:
        copy.wait_send()


def shards(
    link_blocks, inverse_blocks, block_rows, node_of, slot_count, node_diag, first_link, first_diag
):
    groups = lax.axis_size("node")
    width = link_blocks.shape[2]
    ft = jnp.swapaxes(first_link, 1, 2)
    vmem = pl.BlockSpec(memory_space=pltpu.VMEM)
    smem = pl.BlockSpec(memory_space=pltpu.SMEM)
    hbm = pl.BlockSpec(memory_space=pl.ANY)
    dma = pltpu.SemaphoreType.DMA
    waves = []
    for wave in WAVES:
        tile = (len(wave), 8, 128)
        waves += [
            pltpu.VMEM((2, Z, *tile), f32),
            pltpu.VMEM((Z, *tile), f32),
            pltpu.VMEM((Z, *tile), f32),
            pltpu.VMEM(tile, f32),
            pltpu.VMEM(tile, f32),
            pltpu.VMEM((Z, *tile), f32),
        ] + [dma((Z - 1,))] * 4
    return pl.pallas_call(
        functools.partial(kernel, groups),
        out_shape=[
            jax.ShapeDtypeStruct((2, 8, width), f32),
            jax.ShapeDtypeStruct((8, width), f32),
        ],
        in_specs=[smem] * 4 + [hbm] * 2 + [vmem] * 2,
        out_specs=[vmem] * 2,
        scratch_shapes=[
            pltpu.VMEM(link_blocks.shape, f32),
            pltpu.VMEM(inverse_blocks.shape, f32),
            pltpu.VMEM((2, Z, 16, width), f32),
            pltpu.VMEM((K, K, 128, 128), f32),
            pltpu.VMEM((width, width), f32),
            pltpu.VMEM((width, width), f32),
            pltpu.VMEM((4, 8, width), f32),
            pltpu.VMEM((2, groups, 8, width), f32),
            dma((2, link_blocks.shape[0])),
            dma((2, len(WAVES))),
            dma((2, len(WAVES))),
            dma((5,)),
            dma((5,)),
            dma((3, 4)),
            dma((3, 4)),
            dma((2 * groups,)),
            dma((2 * groups,)),
            *waves,
        ],
        compiler_params=pltpu.CompilerParams(
            collective_id=0, has_side_effects=True, vmem_limit_bytes=50 << 20
        ),
        name="schur",
    )(
        block_rows, node_of, slot_count, first_diag,
        link_blocks, inverse_blocks, node_diag, ft,
    )


def solution(mesh):
    in_specs = (
        P(("scen", "node"), None, None),
        P(("scen", "node"), None, None),
        P(("scen", "node")),
        P(("scen", "node")),
        P(("scen", "node")),
        P("node", None),
        P("node", None, "scen"),
        P("scen"),
    )
    out_specs = (P("node", "scen", None), P("scen", None))
    return jax.shard_map(shards, mesh=mesh, in_specs=in_specs, out_specs=out_specs, check_vma=False)
```

```python
import functools

import jax
import jax.numpy as jnp
from jax import lax
from jax.experimental import pallas as pl
from jax.experimental.pallas import tpu as pltpu
from jax.sharding import PartitionSpec as P

f32, bf16 = jnp.float32, jnp.bfloat16
NN = (((1,), (0,)), ((), ()))
NT = (((1,), (1,)), ((), ()))
TN = (((0,), (0,)), ((), ()))
Z = 16
K = 4
WAVES = (
    ((0, 0),),
    ((0, 1), (0, 2), (0, 3)),
    ((1, 1), (1, 2), (1, 3)),
    ((2, 2), (2, 3), (3, 3)),
)
WAVE_OF = {block: (w, i) for w, wave in enumerate(WAVES) for i, block in enumerate(wave)}
FAR_FIRST = (8, 7, 9, 6, 10, 5, 11, 4, 12, 3, 13, 2, 14, 1, 15)
MESH = pl.DeviceIdType.MESH


def split(x):
    high = x.astype(bf16)
    return high, (x - high.astype(f32)).astype(bf16)


def mm(a, b, dims):
    def one(p, q):
        return lax.dot_general(p, q, dims, preferred_element_type=f32)

    return one(a[0], b[0]) + (one(a[0], b[1]) + one(a[1], b[0]))


def sub_row(x, k):
    return jnp.broadcast_to(x[k : k + 1, :], (8, 128))


def lane_col(x, j):
    return jnp.broadcast_to(x[:, j : j + 1], x.shape)


def stack(parts):
    return jnp.concatenate([x[None] for x in parts], 0)


def tree(terms):
    terms = list(terms)
    while len(terms) > 1:
        terms = [
            terms[i] + terms[i + 1] if i + 1 < len(terms) else terms[i]
            for i in range(0, len(terms), 2)
        ]
    return terms[0]


def eliminate(n, hit):
    w = None
    for i in range(8):
        row = jnp.broadcast_to(n[:, i : i + 1, :], (8, 8, 128))
        p = 1.0 / row[i]
        r = lax.rsqrt(row[i])
        m = jnp.where(hit[i], 0.0, n[i])
        c = row * p
        new = jnp.where(hit[i], c, n - m * c)
        parts = [new[:i]] if i else []
        parts.append(jnp.where(hit[i], p, -m * p)[None])
        if i < 7:
            parts.append(new[i + 1 :])
        n = jnp.concatenate(parts, 0)
        mine = jnp.where(hit[i], r, 0.0)[None]
        if i:
            mine = jnp.concatenate([jnp.where(hit[i], row[:i] * r, w), mine], 0)
        w = mine
    return w, n


def diag_block(c):
    sub = lax.broadcasted_iota(jnp.int32, (8, 128), 0)
    lane = lax.broadcasted_iota(jnp.int32, (8, 128), 1)
    hit = [sub == i for i in range(8)]
    u, z = [], []
    e = stack([lane_col(c[0:8], k) for k in range(8)])
    for b in range(16):
        s, rest = 8 * b, 120 - 8 * b
        here = (lane >= s) & (lane < s + 8)
        own = c[:8]
        if rest:
            c = c[8:]
            h = [lane_col(c, s + m) for m in range(8)]
            old = [lane_col(c[:8], s + 8 + k) for k in range(8)]
        w, g = eliminate(e, hit)
        if rest:
            hn = [x[:8] for x in h]
            gc = tree(jnp.broadcast_to(g[:, j : j + 1, :], (8, 8, 128)) * hn[j] for j in range(8))
            e = stack(
                [old[k] - tree(hn[m] * sub_row(gc[m], k) for m in range(8)) for k in range(8)]
            )
        aug = jnp.where(here, jnp.where(lane == s + sub, 1.0, 0.0), own)
        rows = [sub_row(aug, k) for k in range(8)]
        u.append(
            jnp.where(lane >= s + sub, tree(w[k] * sub_row(own, k) for k in range(8)), 0.0)
        )
        z.append(jnp.where(lane < s + 8, tree(w[k] * rows[k] for k in range(8)), 0.0))
        if rest:
            scaled = tree(g[k] * rows[k] for k in range(8))
            wide = lax.broadcasted_iota(jnp.int32, (rest, 128), 1)
            c = jnp.where((wide >= s) & (wide < s + 8), 0.0, c) - tree(
                h[m] * jnp.broadcast_to(scaled[m : m + 1], (rest, 128)) for m in range(8)
            )
    return jnp.concatenate(u, 0), jnp.concatenate(z, 0)


def remote(src, dst, send, recv, to):
    return pltpu.make_async_remote_copy(
        src_ref=src, dst_ref=dst, send_sem=send, recv_sem=recv,
        device_id=to, device_id_type=MESH,
    )


def kernel(
    groups, rows, nodes, count, fd, link_hbm, inverse_hbm, diag, ft, l_out, first_out,
    link, inverse, f_all, a, xt, low, g_own, got, load, twin_s, twin_r, swap_s, swap_r,
    f_s, f_r, end_s, end_r, *wave_refs,
):
    scen = lax.axis_index("scen")
    core, z, x = scen % 2, (scen // 2) % Z, scen // (2 * Z)
    high, kind = z // 4, z % 4
    strip = 4 * kind + high
    group = lax.axis_index("node")
    near_by = (1, 15, 2 + 12 * core)

    def chip(dz):
        return {"scen": (x * Z + (z + dz) % Z) * 2 + core}

    twin = {"scen": scen + 1 - 2 * core}
    across = {"scen": ((1 - x) * Z + z) * 2 + core}
    finals = []
    for c in range(2):
        for n in range(groups):
            if c + n > 0:
                to_core = (core + c) % 2
                to = {"scen": scen - core + to_core, "node": (group + n) % groups}
                finals.append((to_core, to))
    barrier = pltpu.get_barrier_semaphore()
    greet = [chip(d) for d in range(1, Z)] + [across] + [to for _, to in finals]
    for to in greet:
        pl.semaphore_signal(barrier, inc=1, device_id=to, device_id_type=MESH)

    slots = link.shape[0]
    loads = []
    for i in range(slots):
        for n, (src, dst) in enumerate(((link_hbm, link), (inverse_hbm, inverse))):
            loads.append(pltpu.make_async_copy(src.at[i], dst.at[i], load.at[n, i]))
            loads[-1].start()

    per = len(wave_refs) // len(WAVES)
    waves = [wave_refs[per * w : per * w + per] for w in range(len(WAVES))]
    sent = []

    def go(src, dst, send, recv, to):
        copy = remote(src, dst, send, recv, to)
        copy.start()
        sent.append(copy)
        return copy

    def arrive(copies):
        for copy in copies:
            copy.wait_recv()

    for acc, *_ in waves:
        acc[...] = jnp.zeros_like(acc)
    row_id = lax.broadcasted_iota(jnp.int32, (link.shape[1], 1), 0)
    for copy in loads:
        copy.wait()

    def slot(i, carry):
        limit = jnp.where(i < count[0], rows[i], 0)
        masked = jnp.where(row_id < limit, link[i], 0.0)
        first = nodes[i] == 2 * group
        m = split(masked)
        y = split(mm(split(inverse[i]), m, NN))
        for q in range(K):
            lo = 128 * q
            term = mm(
                (m[0][:, lo : lo + 128], m[1][:, lo : lo + 128]),
                (y[0][:, lo:], y[1][:, lo:]),
                TN,
            )
            for j in range(K - q):
                w, p = WAVE_OF[q, q + j]
                acc = waves[w][0]
                part = term[:, 128 * j : 128 * j + 128].reshape(16, 8, 128)
                acc[0, :, p] += jnp.where(first, part, 0.0)
                acc[1, :, p] += jnp.where(first, 0.0, part)
        return carry

    lax.fori_loop(0, slots, slot, 0)
    pl.semaphore_wait(barrier, len(greet))

    twins = []
    for w, (acc, sib, *_) in enumerate(waves):
        twins.append(go(acc.at[1 - core], sib, twin_s.at[w], twin_r.at[w], twin))
        if w == 0:
            f_own = f_all.at[x, high, kind, pl.ds(core * 8, 8), :]
            f_twin = go(ft.at[1 - core], f_own, f_s.at[0], f_r.at[0], twin)
    f_all[x, high, kind, pl.ds(core * 8, 8), :] = ft[core]

    acc, sib, rs, _, mine0, peer0, s0, s_sem, r_sem = waves[0]
    twins[0].wait_recv()
    acc[core] += sib[...]
    direct = []
    for d in FAR_FIRST:
        to = (z + d) % Z
        direct.append(
            go(acc.at[core, 4 * (to % 4) + to // 4], rs.at[z], s_sem.at[d], r_sem.at[d], chip(d))
        )
    rs[z] = acc[core, strip]
    f_twin.wait_recv()
    f_own = f_all.at[x, high, kind]
    f_across = go(f_own, f_own, f_s.at[1], f_r.at[1], across)
    near = {}
    for w in range(1, len(WAVES)):
        acc, sib, rs, half, mine, peer, s_all, s_sem, r_sem = waves[w]
        twins[w].wait_recv()
        acc[core] += sib[...]
        near[w] = [
            go(
                acc.at[core, pl.ds(4 * ((z + d) % 4), 4)], rs.at[pl.ds(4 * i, 4)],
                s_sem.at[i], r_sem.at[i], chip(d),
            )
            for i, d in enumerate(near_by)
        ]
    far = {}
    for w in range(1, len(WAVES)):
        acc, sib, rs, half, mine, peer, s_all, s_sem, r_sem = waves[w]
        arrive(near[w])
        half[...] = (acc[core, pl.ds(4 * kind, 4)] + rs[0:4]) + (rs[4:8] + rs[8:12])
        far[w] = [
            go(half.at[(high + k) % 4], rs.at[11 + k], s_sem.at[2 + k], r_sem.at[2 + k], chip(4 * k))
            for k in (2, 1, 3)
        ]

    f_across.wait_recv()
    piece = f_all.at[:, high, kind]
    f_far = [go(piece, piece, f_s.at[1 + k], f_r.at[1 + k], chip(4 * k)) for k in (2, 1, 3)]

    def swap(w):
        acc, sib, rs, half, mine, peer, *_ = waves[w]
        if w == 0:
            arrive(direct)
            mine[...] = tree(rs[i] for i in range(Z))
        else:
            arrive(far[w])
            mine[...] = (half[high] + rs[12]) + (rs[13] + rs[14])
        return go(mine, peer, swap_s.at[w], swap_r.at[w], across)

    sub = lax.broadcasted_iota(jnp.int32, (8, 128), 0)
    lane = lax.broadcasted_iota(jnp.int32, (8, 128), 1)

    def spread(w, swapped):
        acc, sib, rs, half, mine, peer, s_all, s_sem, r_sem = waves[w]
        swapped.wait_recv()
        s_all[strip] = mine[...] + peer[...]
        for q in range(K):
            if WAVE_OF[q, q][0] == w:
                d = diag[:, 128 * q : 128 * q + 128]
                d = jnp.broadcast_to(jnp.where(core == 0, d[0:1], d[1:2]), (8, 128))
                s_all[strip, WAVE_OF[q, q][1]] += jnp.where(lane == 8 * strip + sub, d, 0.0)
        own = s_all.at[strip]
        if w == 0:
            return [
                go(own, own, s_sem.at[16 + d], r_sem.at[16 + d], chip(d)) for d in FAR_FIRST
            ]
        return [
            go(own, own, s_sem.at[5 + k], r_sem.at[5 + k], chip(4 * k)) for k in (2, 1, 3)
        ]

    def pass_on(w, copies):
        s_all, s_sem, r_sem = waves[w][6:]
        arrive(copies)
        piece = s_all.at[pl.ds(4 * kind, 4)]
        return [
            go(piece, piece, s_sem.at[9 + i], r_sem.at[9 + i], chip(d))
            for i, d in enumerate(near_by)
        ]

    gather0 = spread(0, swap(0))
    swap1 = swap(1)
    swap2 = swap(2)
    gather1 = spread(1, swap1)
    swap3 = swap(3)
    gather2 = spread(2, swap2)
    gather3 = spread(3, swap3)

    def block(i, j):
        w, p = WAVE_OF[i, j]
        return waves[w][6][:, p].reshape(128, 128)

    low[...] = jnp.zeros_like(low)
    us, invs = {}, []

    def solve(q):
        lo = 128 * q
        src = xt
        if q == 0:
            part = f_all[...].reshape(4 * 128, -1)[:, lo : lo + 128]
        else:
            part = xt[:, lo : lo + 128]
        xq = mm(split(part), invs[q], NT)
        xs = split(xq)
        for j in range(q + 1, K):
            hi = 128 * j
            old = f_all[...].reshape(4 * 128, -1)[:, hi : hi + 128] if q == 0 else xt[:, hi : hi + 128]
            xt[:, hi : hi + 128] = old - mm(xs, us[q, j], NN)
        xt[:, lo : lo + 128] = xq

    arrive(gather0)
    for q in range(K):
        lo = 128 * q
        u, inv = diag_block(block(0, 0) if q == 0 else a[q, q])
        low[lo : lo + 128, lo : lo + 128] = u.T
        invs.append(split(inv))
        if q == 0:
            gather1 = pass_on(1, gather1)
            gather2 = pass_on(2, gather2)
            gather3 = pass_on(3, gather3)
            arrive(f_far)
            piece = f_all.at[:, :, kind]
            f_near = [
                go(piece, piece, f_s.at[5 + i], f_r.at[5 + i], chip(d))
                for i, d in enumerate(near_by)
            ]
            arrive(gather1)
        for j in range(q + 1, K):
            v = mm(invs[q], split(block(0, j) if q == 0 else a[q, j]), NN)
            low[128 * j : 128 * j + 128, lo : lo + 128] = v.T
            us[q, j] = split(v)
        if q == 0:
            arrive(gather2)
            for j in range(1, K):
                a[1, j] = block(1, j) - mm(us[0, 1], us[0, j], TN)
        elif q == 1:
            arrive(gather3)
            for i in range(2, K):
                for j in range(i, K):
                    a[i, j] = block(i, j) - (
                        mm(us[0, i], us[0, j], TN) + mm(us[1, i], us[1, j], TN)
                    )
        elif q == 2:
            a[3, 3] -= mm(us[2, 3], us[2, 3], TN)
            arrive(f_near)
            for p in range(3):
                solve(p)
        else:
            solve(3)

    own = pl.multiple_of((x * Z + z) * 16, 16)
    width = first_out.shape[1]
    g_own[0] = low[pl.ds(own, 8), :]
    g_own[1] = low[pl.ds(pl.multiple_of(own + 8, 8), 8), :]
    factor = go(g_own.at[1 - core], l_out.at[core], end_s.at[0], end_r.at[0], twin)
    l_out[core] = g_own[core]
    term = mm(split(xt[pl.ds(own, 16), :]), split(xt[...]), NT)
    g_own[2] = term[:8]
    g_own[3] = term[8:]
    last = [
        go(g_own.at[2 + to_core], got.at[core, group], end_s.at[1 + i], end_r.at[1 + i], to)
        for i, (to_core, to) in enumerate(finals)
    ]
    got[core, group] = g_own[2 + core]
    arrive(last)
    row8 = lax.broadcasted_iota(jnp.int32, (8, width), 0)
    col8 = lax.broadcasted_iota(jnp.int32, (8, width), 1)
    d = jnp.zeros((8, width), f32)
    for i in range(8):
        d = jnp.where(row8 == i, fd[i], d)
    total = tree(got[c, n] for c in range(2) for n in range(groups))
    first_out[...] = total + jnp.where(col8 == scen * 8 + row8, d, 0.0)
    factor.wait_recv()
    for copy in sent:
        copy.wait_send()


def shards(
    link_blocks, inverse_blocks, block_rows, node_of, slot_count, node_diag, first_link, first_diag
):
    groups = lax.axis_size("node")
    width = link_blocks.shape[2]
    ft = jnp.swapaxes(first_link, 1, 2)
    vmem = pl.BlockSpec(memory_space=pltpu.VMEM)
    smem = pl.BlockSpec(memory_space=pltpu.SMEM)
    hbm = pl.BlockSpec(memory_space=pltpu.HBM)
    dma = pltpu.SemaphoreType.DMA
    waves = []
    for wave in WAVES:
        tile = (len(wave), 8, 128)
        waves += [
            pltpu.VMEM((2, Z, *tile), f32),
            pltpu.VMEM((Z, *tile), f32),
            pltpu.VMEM((Z, *tile), f32),
            pltpu.VMEM((4, *tile), f32),
            pltpu.VMEM(tile, f32),
            pltpu.VMEM(tile, f32),
            pltpu.VMEM((Z, *tile), f32),
            dma((2 * Z,)),
            dma((2 * Z,)),
        ]
    return pl.pallas_call(
        functools.partial(kernel, groups),
        out_shape=[
            jax.ShapeDtypeStruct((2, 8, width), f32),
            jax.ShapeDtypeStruct((8, width), f32),
        ],
        in_specs=[smem] * 4 + [hbm] * 2 + [vmem] * 2,
        out_specs=[vmem] * 2,
        scratch_shapes=[
            pltpu.VMEM(link_blocks.shape, f32),
            pltpu.VMEM(inverse_blocks.shape, f32),
            pltpu.VMEM((2, 4, 4, 16, width), f32),
            pltpu.VMEM((K, K, 128, 128), f32),
            pltpu.VMEM((width, width), f32),
            pltpu.VMEM((width, width), f32),
            pltpu.VMEM((4, 8, width), f32),
            pltpu.VMEM((2, groups, 8, width), f32),
            dma((2, link_blocks.shape[0])),
            dma((len(WAVES),)),
            dma((len(WAVES),)),
            dma((len(WAVES),)),
            dma((len(WAVES),)),
            dma((8,)),
            dma((8,)),
            dma((2 * groups,)),
            dma((2 * groups,)),
            *waves,
        ],
        compiler_params=pltpu.CompilerParams(
            collective_id=0, has_side_effects=True, vmem_limit_bytes=50 << 20
        ),
        name="schur",
    )(
        block_rows, node_of, slot_count, first_diag,
        link_blocks, inverse_blocks, node_diag, ft,
    )


def solution(mesh):
    in_specs = (
        P(("scen", "node"), None, None),
        P(("scen", "node"), None, None),
        P(("scen", "node")),
        P(("scen", "node")),
        P(("scen", "node")),
        P("node", None),
        P("node", None, "scen"),
        P("scen"),
    )
    out_specs = (P("node", "scen", None), P("scen", None))
    return jax.shard_map(shards, mesh=mesh, in_specs=in_specs, out_specs=out_specs, check_vma=False)
```

```python
import functools

import jax
import jax.numpy as jnp
from jax import lax
from jax.experimental import pallas as pl
from jax.experimental.pallas import tpu as pltpu
from jax.sharding import PartitionSpec as P

f32, bf16 = jnp.float32, jnp.bfloat16
NN = (((1,), (0,)), ((), ()))
NT = (((1,), (1,)), ((), ()))
TN = (((0,), (0,)), ((), ()))
Z = 16
K = 4
WAVES = (
    ((0, 0),),
    ((0, 1), (0, 2), (0, 3), (1, 1)),
    ((1, 2), (1, 3), (2, 2), (2, 3), (3, 3)),
)
WAVE_OF = {block: (w, i) for w, wave in enumerate(WAVES) for i, block in enumerate(wave)}
DIRECT = 1
FAR_FIRST = (8, 7, 9, 6, 10, 5, 11, 4, 12, 3, 13, 2, 14, 1, 15)
MESH = pl.DeviceIdType.MESH


def split(x):
    high = x.astype(bf16)
    return high, (x - high.astype(f32)).astype(bf16)


def mm(a, b, dims):
    def one(p, q):
        return lax.dot_general(p, q, dims, preferred_element_type=f32)

    return one(a[0], b[0]) + (one(a[0], b[1]) + one(a[1], b[0]))


def sub_row(x, k):
    return jnp.broadcast_to(x[k : k + 1, :], (8, 128))


def lane_col(x, j):
    return jnp.broadcast_to(x[:, j : j + 1], x.shape)


def stack(parts):
    return jnp.concatenate([x[None] for x in parts], 0)


def tree(terms):
    terms = list(terms)
    while len(terms) > 1:
        terms = [
            terms[i] + terms[i + 1] if i + 1 < len(terms) else terms[i]
            for i in range(0, len(terms), 2)
        ]
    return terms[0]


def eliminate(n, hit):
    w = None
    for i in range(8):
        row = jnp.broadcast_to(n[:, i : i + 1, :], (8, 8, 128))
        p = 1.0 / row[i]
        r = lax.rsqrt(row[i])
        m = jnp.where(hit[i], 0.0, n[i])
        c = row * p
        new = jnp.where(hit[i], c, n - m * c)
        parts = [new[:i]] if i else []
        parts.append(jnp.where(hit[i], p, -m * p)[None])
        if i < 7:
            parts.append(new[i + 1 :])
        n = jnp.concatenate(parts, 0)
        mine = jnp.where(hit[i], r, 0.0)[None]
        if i:
            mine = jnp.concatenate([jnp.where(hit[i], row[:i] * r, w), mine], 0)
        w = mine
    return w, n


def diag_block(c):
    sub = lax.broadcasted_iota(jnp.int32, (8, 128), 0)
    lane = lax.broadcasted_iota(jnp.int32, (8, 128), 1)
    hit = [sub == i for i in range(8)]
    u, z = [], []
    e = stack([lane_col(c[0:8], k) for k in range(8)])
    for b in range(16):
        s, rest = 8 * b, 120 - 8 * b
        here = (lane >= s) & (lane < s + 8)
        own = c[:8]
        if rest:
            c = c[8:]
            h = [lane_col(c, s + m) for m in range(8)]
            old = [lane_col(c[:8], s + 8 + k) for k in range(8)]
        w, g = eliminate(e, hit)
        if rest:
            hn = [x[:8] for x in h]
            gc = tree(jnp.broadcast_to(g[:, j : j + 1, :], (8, 8, 128)) * hn[j] for j in range(8))
            e = stack(
                [old[k] - tree(hn[m] * sub_row(gc[m], k) for m in range(8)) for k in range(8)]
            )
        aug = jnp.where(here, jnp.where(lane == s + sub, 1.0, 0.0), own)
        rows = [sub_row(aug, k) for k in range(8)]
        u.append(
            jnp.where(lane >= s + sub, tree(w[k] * sub_row(own, k) for k in range(8)), 0.0)
        )
        z.append(jnp.where(lane < s + 8, tree(w[k] * rows[k] for k in range(8)), 0.0))
        if rest:
            scaled = tree(g[k] * rows[k] for k in range(8))
            wide = lax.broadcasted_iota(jnp.int32, (rest, 128), 1)
            c = jnp.where((wide >= s) & (wide < s + 8), 0.0, c) - tree(
                h[m] * jnp.broadcast_to(scaled[m : m + 1], (rest, 128)) for m in range(8)
            )
    return jnp.concatenate(u, 0), jnp.concatenate(z, 0)


def remote(src, dst, send, recv, to):
    return pltpu.make_async_remote_copy(
        src_ref=src, dst_ref=dst, send_sem=send, recv_sem=recv,
        device_id=to, device_id_type=MESH,
    )


def kernel(
    groups, rows, nodes, count, fd, link, inverse, diag, ft, l_out, first_out,
    f_all, f_peer, a, xt, low, l_own, g_own, got, twin_s, twin_r, swap_s, swap_r,
    f_s, f_r, end_s, end_r, *wave_refs,
):
    scen = lax.axis_index("scen")
    core, z, x = scen % 2, (scen // 2) % Z, scen // (2 * Z)
    high, kind = z // 4, z % 4
    strip = 4 * kind + high
    group = lax.axis_index("node")
    near_by = (1, 15, 2 + 12 * core)

    def chip(dz):
        return {"scen": (x * Z + (z + dz) % Z) * 2 + core}

    twin = {"scen": scen + 1 - 2 * core}
    across = {"scen": ((1 - x) * Z + z) * 2 + core}
    finals = []
    for dx in range(2):
        for c in range(2):
            for n in range(groups):
                if dx + c + n > 0:
                    to_core, to_x = (core + c) % 2, (x + dx) % 2
                    to = {"scen": (to_x * Z + z) * 2 + to_core, "node": (group + n) % groups}
                    finals.append((dx, to_core, to))
    barrier = pltpu.get_barrier_semaphore()
    greet = [chip(d) for d in range(1, Z)] + [to for *_, to in finals]
    for to in greet:
        pl.semaphore_signal(barrier, inc=1, device_id=to, device_id_type=MESH)

    slots = link.shape[0]
    per = len(wave_refs) // len(WAVES)
    waves = [wave_refs[per * w : per * w + per] for w in range(len(WAVES))]
    sent = []

    def go(src, dst, send, recv, to):
        copy = remote(src, dst, send, recv, to)
        copy.start()
        sent.append(copy)
        return copy

    def arrive(copies):
        for copy in copies:
            copy.wait_recv()

    for acc, *_ in waves:
        acc[...] = jnp.zeros_like(acc)
    row_id = lax.broadcasted_iota(jnp.int32, (link.shape[1], 1), 0)

    def slot(i, carry):
        limit = jnp.where(i < count[0], rows[i], 0)
        masked = jnp.where(row_id < limit, link[i], 0.0)
        first = nodes[i] == 2 * group
        m = split(masked)
        y = split(mm(split(inverse[i]), m, NN))
        for q in range(K):
            lo = 128 * q
            term = mm(
                (m[0][:, lo : lo + 128], m[1][:, lo : lo + 128]),
                (y[0][:, lo:], y[1][:, lo:]),
                TN,
            )
            for j in range(K - q):
                w, p = WAVE_OF[q, q + j]
                acc = waves[w][0]
                part = term[:, 128 * j : 128 * j + 128].reshape(16, 8, 128)
                acc[0, :, p] += jnp.where(first, part, 0.0)
                acc[1, :, p] += jnp.where(first, 0.0, part)
        return carry

    lax.fori_loop(0, slots, slot, 0)
    pl.semaphore_wait(barrier, len(greet))

    twins = []
    for w, (acc, sib, *_) in enumerate(waves):
        twins.append(go(acc.at[1 - core], sib, twin_s.at[w], twin_r.at[w], twin))
        if w == 0:
            f_own = f_all.at[high, kind, pl.ds(core * 8, 8), :]
            f_twin = go(ft.at[1 - core], f_own, f_s.at[0], f_r.at[0], twin)
    f_all[high, kind, pl.ds(core * 8, 8), :] = ft[core]

    if DIRECT:
        acc, sib, rs, _, mine0, peer0, s0, s_sem, r_sem = waves[0]
        twins[0].wait_recv()
        acc[core] += sib[...]
        direct = []
        for d in FAR_FIRST:
            to = (z + d) % Z
            direct.append(
                go(acc.at[core, 4 * (to % 4) + to // 4], rs.at[z], s_sem.at[d], r_sem.at[d], chip(d))
            )
        rs[z] = acc[core, strip]
    f_twin.wait_recv()
    f_across = go(f_all.at[high, kind], f_peer, f_s.at[1], f_r.at[1], across)
    near = {}
    for w in range(DIRECT, len(WAVES)):
        acc, sib, rs, half, mine, peer, s_all, s_sem, r_sem = waves[w]
        twins[w].wait_recv()
        acc[core] += sib[...]
        near[w] = [
            go(
                acc.at[core, pl.ds(4 * ((z + d) % 4), 4)], rs.at[pl.ds(4 * i, 4)],
                s_sem.at[i], r_sem.at[i], chip(d),
            )
            for i, d in enumerate(near_by)
        ]
    far = {}
    for w in range(DIRECT, len(WAVES)):
        acc, sib, rs, half, mine, peer, s_all, s_sem, r_sem = waves[w]
        arrive(near[w])
        half[...] = (acc[core, pl.ds(4 * kind, 4)] + rs[0:4]) + (rs[4:8] + rs[8:12])
        far[w] = [
            go(half.at[(high + k) % 4], rs.at[11 + k], s_sem.at[2 + k], r_sem.at[2 + k], chip(4 * k))
            for k in (2, 1, 3)
        ]

    piece = f_all.at[high, kind]
    f_far = [go(piece, piece, f_s.at[1 + k], f_r.at[1 + k], chip(4 * k)) for k in (2, 1, 3)]

    def swap(w):
        acc, sib, rs, half, mine, peer, *_ = waves[w]
        if w < DIRECT:
            arrive(direct)
            mine[...] = tree(rs[i] for i in range(Z))
        else:
            arrive(far[w])
            mine[...] = (half[high] + rs[12]) + (rs[13] + rs[14])
        return go(mine, peer, swap_s.at[w], swap_r.at[w], across)

    sub = lax.broadcasted_iota(jnp.int32, (8, 128), 0)
    lane = lax.broadcasted_iota(jnp.int32, (8, 128), 1)

    def spread(w, swapped):
        acc, sib, rs, half, mine, peer, s_all, s_sem, r_sem = waves[w]
        swapped.wait_recv()
        s_all[strip] = mine[...] + peer[...]
        for q in range(K):
            if WAVE_OF[q, q][0] == w:
                d = diag[:, 128 * q : 128 * q + 128]
                d = jnp.broadcast_to(jnp.where(core == 0, d[0:1], d[1:2]), (8, 128))
                s_all[strip, WAVE_OF[q, q][1]] += jnp.where(lane == 8 * strip + sub, d, 0.0)
        own = s_all.at[strip]
        if w < DIRECT:
            return [
                go(own, own, s_sem.at[16 + d], r_sem.at[16 + d], chip(d)) for d in FAR_FIRST
            ]
        return [
            go(own, own, s_sem.at[5 + k], r_sem.at[5 + k], chip(4 * k)) for k in (2, 1, 3)
        ]

    def pass_on(w, copies):
        s_all, s_sem, r_sem = waves[w][6:]
        arrive(copies)
        piece = s_all.at[pl.ds(4 * kind, 4)]
        return [
            go(piece, piece, s_sem.at[9 + i], r_sem.at[9 + i], chip(d))
            for i, d in enumerate(near_by)
        ]

    gathers = {}
    if DIRECT:
        gathers[0] = spread(0, swap(0))
    swaps = {}
    for w in range(DIRECT, len(WAVES)):
        swaps[w] = swap(w)
        if w - 1 in swaps:
            gathers[w - 1] = spread(w - 1, swaps[w - 1])
    gathers[w] = spread(w, swaps[w])

    def block(i, j):
        w, p = WAVE_OF[i, j]
        return waves[w][6][:, p].reshape(128, 128)

    low[...] = jnp.zeros_like(low)
    us, invs = {}, []
    own_half = xt.shape[0] - 16

    def columns(lo):
        half = f_all[...].reshape(own_half, -1)[:, lo : lo + 128]
        return jnp.concatenate([half, f_peer[:, lo : lo + 128]], 0)

    def solve(q):
        lo = 128 * q
        xq = mm(split(columns(lo) if q == 0 else xt[:, lo : lo + 128]), invs[q], NT)
        xs = split(xq)
        for j in range(q + 1, K):
            hi = 128 * j
            old = columns(hi) if q == 0 else xt[:, hi : hi + 128]
            xt[:, hi : hi + 128] = old - mm(xs, us[q, j], NN)
        xt[:, lo : lo + 128] = xq

    done = set()

    def ready(row):
        for j in range(row, K):
            w = WAVE_OF[row, j][0]
            if w not in done:
                done.add(w)
                arrive(gathers[w])

    if not DIRECT:
        gathers[0] = pass_on(0, gathers[0])
    arrive(gathers[0])
    done.add(0)
    for q in range(K):
        lo = 128 * q
        u, inv = diag_block(block(0, 0) if q == 0 else a[q, q])
        low[lo : lo + 128, lo : lo + 128] = u.T
        invs.append(split(inv))
        if q == 0:
            for w in range(1, len(WAVES)):
                gathers[w] = pass_on(w, gathers[w])
            arrive(f_far)
            piece = f_all.at[:, kind]
            f_near = [
                go(piece, piece, f_s.at[5 + i], f_r.at[5 + i], chip(d))
                for i, d in enumerate(near_by)
            ]
            ready(0)
        for j in range(q + 1, K):
            v = mm(invs[q], split(block(0, j) if q == 0 else a[q, j]), NN)
            low[128 * j : 128 * j + 128, lo : lo + 128] = v.T
            us[q, j] = split(v)
        if q == 0:
            ready(1)
            for j in range(1, K):
                a[1, j] = block(1, j) - mm(us[0, 1], us[0, j], TN)
        elif q == 1:
            ready(2)
            ready(3)
            for i in range(2, K):
                for j in range(i, K):
                    a[i, j] = block(i, j) - (
                        mm(us[0, i], us[0, j], TN) + mm(us[1, i], us[1, j], TN)
                    )
        elif q == 2:
            a[3, 3] -= mm(us[2, 3], us[2, 3], TN)
            arrive(f_near + [f_across])
            for p in range(3):
                solve(p)
        else:
            solve(3)

    own = pl.multiple_of((x * Z + z) * 16, 16)
    width = first_out.shape[1]
    l_own[0] = low[pl.ds(own, 8), :]
    l_own[1] = low[pl.ds(pl.multiple_of(own + 8, 8), 8), :]
    factor = go(l_own.at[1 - core], l_out.at[core], end_s.at[0], end_r.at[0], twin)
    l_out[core] = l_own[core]
    wanted = jnp.concatenate([xt[pl.ds(pl.multiple_of(16 * z, 16), 16), :], xt[own_half:, :]], 0)
    term = mm(split(wanted), split(xt[:own_half, :]), NT)
    for dx in range(2):
        for c in range(2):
            lo = 16 * dx + 8 * c
            g_own[dx, c] = term[lo : lo + 8]
    last = [
        go(g_own.at[dx, to_core], got.at[x, core, group], end_s.at[1 + i], end_r.at[1 + i], to)
        for i, (dx, to_core, to) in enumerate(finals)
    ]
    got[x, core, group] = g_own[0, core]
    arrive(last)
    row8 = lax.broadcasted_iota(jnp.int32, (8, width), 0)
    col8 = lax.broadcasted_iota(jnp.int32, (8, width), 1)
    d = jnp.zeros((8, width), f32)
    for i in range(8):
        d = jnp.where(row8 == i, fd[i], d)
    total = jnp.concatenate(
        [tree(got[h, c, n] for c in range(2) for n in range(groups)) for h in range(2)], 1
    )
    first_out[...] = total + jnp.where(col8 == scen * 8 + row8, d, 0.0)
    factor.wait_recv()
    for copy in sent:
        copy.wait_send()


def shards(
    link_blocks, inverse_blocks, block_rows, node_of, slot_count, node_diag, first_link, first_diag
):
    groups = lax.axis_size("node")
    width = link_blocks.shape[2]
    ft = jnp.swapaxes(first_link, 1, 2)
    vmem = pl.BlockSpec(memory_space=pltpu.VMEM)
    smem = pl.BlockSpec(memory_space=pltpu.SMEM)
    dma = pltpu.SemaphoreType.DMA
    waves = []
    for wave in WAVES:
        tile = (len(wave), 8, 128)
        waves += [
            pltpu.VMEM((2, Z, *tile), f32),
            pltpu.VMEM((Z, *tile), f32),
            pltpu.VMEM((Z, *tile), f32),
            pltpu.VMEM((4, *tile), f32),
            pltpu.VMEM(tile, f32),
            pltpu.VMEM(tile, f32),
            pltpu.VMEM((Z, *tile), f32),
            dma((2 * Z,)),
            dma((2 * Z,)),
        ]
    return pl.pallas_call(
        functools.partial(kernel, groups),
        out_shape=[
            jax.ShapeDtypeStruct((2, 8, width), f32),
            jax.ShapeDtypeStruct((8, width), f32),
        ],
        in_specs=[smem] * 4 + [vmem] * 4,
        out_specs=[vmem] * 2,
        scratch_shapes=[
            pltpu.VMEM((4, 4, 16, width), f32),
            pltpu.VMEM((16, width), f32),
            pltpu.VMEM((K, K, 128, 128), f32),
            pltpu.VMEM((width // 2 + 16, width), f32),
            pltpu.VMEM((width, width), f32),
            pltpu.VMEM((2, 8, width), f32),
            pltpu.VMEM((2, 2, 8, width // 2), f32),
            pltpu.VMEM((2, 2, groups, 8, width // 2), f32),
            dma((len(WAVES),)),
            dma((len(WAVES),)),
            dma((len(WAVES),)),
            dma((len(WAVES),)),
            dma((8,)),
            dma((8,)),
            dma((4 * groups,)),
            dma((4 * groups,)),
            *waves,
        ],
        compiler_params=pltpu.CompilerParams(
            collective_id=0, has_side_effects=True, vmem_limit_bytes=50 << 20
        ),
        name="schur",
    )(
        block_rows, node_of, slot_count, first_diag,
        link_blocks, inverse_blocks, node_diag, ft,
    )


def solution(mesh):
    in_specs = (
        P(("scen", "node"), None, None),
        P(("scen", "node"), None, None),
        P(("scen", "node")),
        P(("scen", "node")),
        P(("scen", "node")),
        P("node", None),
        P("node", None, "scen"),
        P("scen"),
    )
    out_specs = (P("node", "scen", None), P("scen", None))
    return jax.shard_map(shards, mesh=mesh, in_specs=in_specs, out_specs=out_specs, check_vma=False)
```

```python
import functools

import jax
import jax.numpy as jnp
from jax import lax
from jax.experimental import pallas as pl
from jax.experimental.pallas import tpu as pltpu
from jax.sharding import PartitionSpec as P

f32, bf16 = jnp.float32, jnp.bfloat16
NN = (((1,), (0,)), ((), ()))
NT = (((1,), (1,)), ((), ()))
TN = (((0,), (0,)), ((), ()))
Z = 16
K = 4
WAVES = (
    ((0, 0),),
    ((0, 1), (0, 2), (0, 3), (1, 1)),
    ((1, 2), (1, 3), (2, 2), (2, 3), (3, 3)),
)
WAVE_OF = {block: (w, i) for w, wave in enumerate(WAVES) for i, block in enumerate(wave)}
DIRECT = 1
FAR_FIRST = (8, 7, 9, 6, 10, 5, 11, 4, 12, 3, 13, 2, 14, 1, 15)
MESH = pl.DeviceIdType.MESH


def split(x):
    high = x.astype(bf16)
    return high, (x - high.astype(f32)).astype(bf16)


def mm(a, b, dims):
    def one(p, q):
        return lax.dot_general(p, q, dims, preferred_element_type=f32)

    return one(a[0], b[0]) + (one(a[0], b[1]) + one(a[1], b[0]))


def sub_row(x, k):
    return jnp.broadcast_to(x[k : k + 1, :], (8, 128))


def lane_col(x, j):
    return jnp.broadcast_to(x[:, j : j + 1], x.shape)


def stack(parts):
    return jnp.concatenate([x[None] for x in parts], 0)


def tree(terms):
    terms = list(terms)
    while len(terms) > 1:
        terms = [
            terms[i] + terms[i + 1] if i + 1 < len(terms) else terms[i]
            for i in range(0, len(terms), 2)
        ]
    return terms[0]


def eliminate(n, hit):
    w = None
    for i in range(8):
        row = jnp.broadcast_to(n[:, i : i + 1, :], (8, 8, 128))
        p = 1.0 / row[i]
        r = lax.rsqrt(row[i])
        m = jnp.where(hit[i], 0.0, n[i])
        c = row * p
        new = jnp.where(hit[i], c, n - m * c)
        parts = [new[:i]] if i else []
        parts.append(jnp.where(hit[i], p, -m * p)[None])
        if i < 7:
            parts.append(new[i + 1 :])
        n = jnp.concatenate(parts, 0)
        mine = jnp.where(hit[i], r, 0.0)[None]
        if i:
            mine = jnp.concatenate([jnp.where(hit[i], row[:i] * r, w), mine], 0)
        w = mine
    return w, n


def diag_block(c):
    sub = lax.broadcasted_iota(jnp.int32, (8, 128), 0)
    lane = lax.broadcasted_iota(jnp.int32, (8, 128), 1)
    hit = [sub == i for i in range(8)]
    u, z = [], []
    e = stack([lane_col(c[0:8], k) for k in range(8)])
    for b in range(16):
        s, rest = 8 * b, 120 - 8 * b
        here = (lane >= s) & (lane < s + 8)
        own = c[:8]
        if rest:
            c = c[8:]
            h = [lane_col(c, s + m) for m in range(8)]
            old = [lane_col(c[:8], s + 8 + k) for k in range(8)]
        w, g = eliminate(e, hit)
        if rest:
            hn = [x[:8] for x in h]
            gc = tree(jnp.broadcast_to(g[:, j : j + 1, :], (8, 8, 128)) * hn[j] for j in range(8))
            e = stack(
                [old[k] - tree(hn[m] * sub_row(gc[m], k) for m in range(8)) for k in range(8)]
            )
        aug = jnp.where(here, jnp.where(lane == s + sub, 1.0, 0.0), own)
        rows = [sub_row(aug, k) for k in range(8)]
        u.append(
            jnp.where(lane >= s + sub, tree(w[k] * sub_row(own, k) for k in range(8)), 0.0)
        )
        z.append(jnp.where(lane < s + 8, tree(w[k] * rows[k] for k in range(8)), 0.0))
        if rest:
            scaled = tree(g[k] * rows[k] for k in range(8))
            wide = lax.broadcasted_iota(jnp.int32, (rest, 128), 1)
            c = jnp.where((wide >= s) & (wide < s + 8), 0.0, c) - tree(
                h[m] * jnp.broadcast_to(scaled[m : m + 1], (rest, 128)) for m in range(8)
            )
    return jnp.concatenate(u, 0), jnp.concatenate(z, 0)


def remote(src, dst, send, recv, to):
    return pltpu.make_async_remote_copy(
        src_ref=src, dst_ref=dst, send_sem=send, recv_sem=recv,
        device_id=to, device_id_type=MESH,
    )


def kernel(
    groups, rows, nodes, count, fd, link_hbm, inverse_hbm, diag, ft, l_out, first_out,
    link, inverse, load, f_all, f_peer, a, xt, low, l_own, g_own, got, twin_s, twin_r, swap_s, swap_r,
    f_s, f_r, end_s, end_r, *wave_refs,
):
    scen = lax.axis_index("scen")
    core, z, x = scen % 2, (scen // 2) % Z, scen // (2 * Z)
    high, kind = z // 4, z % 4
    strip = 4 * kind + high
    group = lax.axis_index("node")
    near_by = (1, 15, 2 + 12 * core)

    def chip(dz):
        return {"scen": (x * Z + (z + dz) % Z) * 2 + core}

    twin = {"scen": scen + 1 - 2 * core}
    across = {"scen": ((1 - x) * Z + z) * 2 + core}
    finals = []
    for dx in range(2):
        for c in range(2):
            for n in range(groups):
                if dx + c + n > 0:
                    to_core, to_x = (core + c) % 2, (x + dx) % 2
                    to = {"scen": (to_x * Z + z) * 2 + to_core, "node": (group + n) % groups}
                    finals.append((dx, to_core, to))
    barrier = pltpu.get_barrier_semaphore()
    greet = [chip(d) for d in range(1, Z)] + [to for *_, to in finals]
    for to in greet:
        pl.semaphore_signal(barrier, inc=1, device_id=to, device_id_type=MESH)

    slots = link.shape[0]
    loads = []
    for i in range(slots):
        for n, (src, dst) in enumerate(((link_hbm, link), (inverse_hbm, inverse))):
            loads.append(pltpu.make_async_copy(src.at[i], dst.at[i], load.at[n, i]))
            loads[-1].start()

    per = len(wave_refs) // len(WAVES)
    waves = [wave_refs[per * w : per * w + per] for w in range(len(WAVES))]
    sent = []

    def go(src, dst, send, recv, to):
        copy = remote(src, dst, send, recv, to)
        copy.start()
        sent.append(copy)
        return copy

    def arrive(copies):
        for copy in copies:
            copy.wait_recv()

    for acc, *_ in waves:
        acc[...] = jnp.zeros_like(acc)
    row_id = lax.broadcasted_iota(jnp.int32, (link.shape[1], 1), 0)
    for copy in loads:
        copy.wait()

    def slot(i, carry):
        limit = jnp.where(i < count[0], rows[i], 0)
        masked = jnp.where(row_id < limit, link[i], 0.0)
        first = nodes[i] == 2 * group
        m = split(masked)
        y = split(mm(split(inverse[i]), m, NN))
        for q in range(K):
            lo = 128 * q
            term = mm(
                (m[0][:, lo : lo + 128], m[1][:, lo : lo + 128]),
                (y[0][:, lo:], y[1][:, lo:]),
                TN,
            )
            for j in range(K - q):
                w, p = WAVE_OF[q, q + j]
                acc = waves[w][0]
                part = term[:, 128 * j : 128 * j + 128].reshape(16, 8, 128)
                acc[0, :, p] += jnp.where(first, part, 0.0)
                acc[1, :, p] += jnp.where(first, 0.0, part)
        return carry

    lax.fori_loop(0, slots, slot, 0)
    pl.semaphore_wait(barrier, len(greet))

    twins = []
    for w, (acc, sib, *_) in enumerate(waves):
        twins.append(go(acc.at[1 - core], sib, twin_s.at[w], twin_r.at[w], twin))
        if w == 0:
            f_own = f_all.at[high, kind, pl.ds(core * 8, 8), :]
            f_twin = go(ft.at[1 - core], f_own, f_s.at[0], f_r.at[0], twin)
    f_all[high, kind, pl.ds(core * 8, 8), :] = ft[core]

    if DIRECT:
        acc, sib, rs, _, mine0, peer0, s0, s_sem, r_sem = waves[0]
        twins[0].wait_recv()
        acc[core] += sib[...]
        direct = []
        for d in FAR_FIRST:
            to = (z + d) % Z
            direct.append(
                go(acc.at[core, 4 * (to % 4) + to // 4], rs.at[z], s_sem.at[d], r_sem.at[d], chip(d))
            )
        rs[z] = acc[core, strip]
    f_twin.wait_recv()
    f_across = go(f_all.at[high, kind], f_peer, f_s.at[1], f_r.at[1], across)
    near = {}
    for w in range(DIRECT, len(WAVES)):
        acc, sib, rs, half, mine, peer, s_all, s_sem, r_sem = waves[w]
        twins[w].wait_recv()
        acc[core] += sib[...]
        near[w] = [
            go(
                acc.at[core, pl.ds(4 * ((z + d) % 4), 4)], rs.at[pl.ds(4 * i, 4)],
                s_sem.at[i], r_sem.at[i], chip(d),
            )
            for i, d in enumerate(near_by)
        ]
    far = {}
    for w in range(DIRECT, len(WAVES)):
        acc, sib, rs, half, mine, peer, s_all, s_sem, r_sem = waves[w]
        arrive(near[w])
        half[...] = (acc[core, pl.ds(4 * kind, 4)] + rs[0:4]) + (rs[4:8] + rs[8:12])
        far[w] = [
            go(half.at[(high + k) % 4], rs.at[11 + k], s_sem.at[2 + k], r_sem.at[2 + k], chip(4 * k))
            for k in (2, 1, 3)
        ]

    piece = f_all.at[high, kind]
    f_far = [go(piece, piece, f_s.at[1 + k], f_r.at[1 + k], chip(4 * k)) for k in (2, 1, 3)]

    def swap(w):
        acc, sib, rs, half, mine, peer, *_ = waves[w]
        if w < DIRECT:
            arrive(direct)
            mine[...] = tree(rs[i] for i in range(Z))
        else:
            arrive(far[w])
            mine[...] = (half[high] + rs[12]) + (rs[13] + rs[14])
        return go(mine, peer, swap_s.at[w], swap_r.at[w], across)

    sub = lax.broadcasted_iota(jnp.int32, (8, 128), 0)
    lane = lax.broadcasted_iota(jnp.int32, (8, 128), 1)

    def spread(w, swapped):
        acc, sib, rs, half, mine, peer, s_all, s_sem, r_sem = waves[w]
        swapped.wait_recv()
        s_all[strip] = mine[...] + peer[...]
        for q in range(K):
            if WAVE_OF[q, q][0] == w:
                d = diag[:, 128 * q : 128 * q + 128]
                d = jnp.broadcast_to(jnp.where(core == 0, d[0:1], d[1:2]), (8, 128))
                s_all[strip, WAVE_OF[q, q][1]] += jnp.where(lane == 8 * strip + sub, d, 0.0)
        own = s_all.at[strip]
        if w < DIRECT:
            return [
                go(own, own, s_sem.at[16 + d], r_sem.at[16 + d], chip(d)) for d in FAR_FIRST
            ]
        return [
            go(own, own, s_sem.at[5 + k], r_sem.at[5 + k], chip(4 * k)) for k in (2, 1, 3)
        ]

    def pass_on(w, copies):
        s_all, s_sem, r_sem = waves[w][6:]
        arrive(copies)
        piece = s_all.at[pl.ds(4 * kind, 4)]
        return [
            go(piece, piece, s_sem.at[9 + i], r_sem.at[9 + i], chip(d))
            for i, d in enumerate(near_by)
        ]

    gathers = {}
    if DIRECT:
        gathers[0] = spread(0, swap(0))
    swaps = {}
    for w in range(DIRECT, len(WAVES)):
        swaps[w] = swap(w)
        if w - 1 in swaps:
            gathers[w - 1] = spread(w - 1, swaps[w - 1])
    gathers[w] = spread(w, swaps[w])

    def block(i, j):
        w, p = WAVE_OF[i, j]
        return waves[w][6][:, p].reshape(128, 128)

    low[...] = jnp.zeros_like(low)
    us, invs = {}, []
    own_half = xt.shape[0] - 16

    def columns(lo):
        half = f_all[...].reshape(own_half, -1)[:, lo : lo + 128]
        return jnp.concatenate([half, f_peer[:, lo : lo + 128]], 0)

    def solve(q):
        lo = 128 * q
        xq = mm(split(columns(lo) if q == 0 else xt[:, lo : lo + 128]), invs[q], NT)
        xs = split(xq)
        for j in range(q + 1, K):
            hi = 128 * j
            old = columns(hi) if q == 0 else xt[:, hi : hi + 128]
            xt[:, hi : hi + 128] = old - mm(xs, us[q, j], NN)
        xt[:, lo : lo + 128] = xq

    done = set()

    def ready(row):
        for j in range(row, K):
            w = WAVE_OF[row, j][0]
            if w not in done:
                done.add(w)
                arrive(gathers[w])

    if not DIRECT:
        gathers[0] = pass_on(0, gathers[0])
    arrive(gathers[0])
    done.add(0)
    for q in range(K):
        lo = 128 * q
        u, inv = diag_block(block(0, 0) if q == 0 else a[q, q])
        low[lo : lo + 128, lo : lo + 128] = u.T
        invs.append(split(inv))
        if q == 0:
            for w in range(1, len(WAVES)):
                gathers[w] = pass_on(w, gathers[w])
            arrive(f_far)
            piece = f_all.at[:, kind]
            f_near = [
                go(piece, piece, f_s.at[5 + i], f_r.at[5 + i], chip(d))
                for i, d in enumerate(near_by)
            ]
            ready(0)
        for j in range(q + 1, K):
            v = mm(invs[q], split(block(0, j) if q == 0 else a[q, j]), NN)
            low[128 * j : 128 * j + 128, lo : lo + 128] = v.T
            us[q, j] = split(v)
        if q == 0:
            ready(1)
            for j in range(1, K):
                a[1, j] = block(1, j) - mm(us[0, 1], us[0, j], TN)
        elif q == 1:
            ready(2)
            ready(3)
            for i in range(2, K):
                for j in range(i, K):
                    a[i, j] = block(i, j) - (
                        mm(us[0, i], us[0, j], TN) + mm(us[1, i], us[1, j], TN)
                    )
        elif q == 2:
            a[3, 3] -= mm(us[2, 3], us[2, 3], TN)
            arrive(f_near + [f_across])
            for p in range(3):
                solve(p)
        else:
            solve(3)

    own = pl.multiple_of((x * Z + z) * 16, 16)
    width = first_out.shape[1]
    l_own[0] = low[pl.ds(own, 8), :]
    l_own[1] = low[pl.ds(pl.multiple_of(own + 8, 8), 8), :]
    factor = go(l_own.at[1 - core], l_out.at[core], end_s.at[0], end_r.at[0], twin)
    l_out[core] = l_own[core]
    wanted = jnp.concatenate([xt[pl.ds(pl.multiple_of(16 * z, 16), 16), :], xt[own_half:, :]], 0)
    term = mm(split(wanted), split(xt[:own_half, :]), NT)
    for dx in range(2):
        for c in range(2):
            lo = 16 * dx + 8 * c
            g_own[dx, c] = term[lo : lo + 8]
    last = [
        go(g_own.at[dx, to_core], got.at[x, core, group], end_s.at[1 + i], end_r.at[1 + i], to)
        for i, (dx, to_core, to) in enumerate(finals)
    ]
    got[x, core, group] = g_own[0, core]
    arrive(last)
    row8 = lax.broadcasted_iota(jnp.int32, (8, width), 0)
    col8 = lax.broadcasted_iota(jnp.int32, (8, width), 1)
    d = jnp.zeros((8, width), f32)
    for i in range(8):
        d = jnp.where(row8 == i, fd[i], d)
    total = jnp.concatenate(
        [tree(got[h, c, n] for c in range(2) for n in range(groups)) for h in range(2)], 1
    )
    first_out[...] = total + jnp.where(col8 == scen * 8 + row8, d, 0.0)
    factor.wait_recv()
    for copy in sent:
        copy.wait_send()


def shards(
    link_blocks, inverse_blocks, block_rows, node_of, slot_count, node_diag, first_link, first_diag
):
    groups = lax.axis_size("node")
    width = link_blocks.shape[2]
    ft = jnp.swapaxes(first_link, 1, 2)
    vmem = pl.BlockSpec(memory_space=pltpu.VMEM)
    smem = pl.BlockSpec(memory_space=pltpu.SMEM)
    hbm = pl.BlockSpec(memory_space=pltpu.HBM)
    dma = pltpu.SemaphoreType.DMA
    waves = []
    for wave in WAVES:
        tile = (len(wave), 8, 128)
        waves += [
            pltpu.VMEM((2, Z, *tile), f32),
            pltpu.VMEM((Z, *tile), f32),
            pltpu.VMEM((Z, *tile), f32),
            pltpu.VMEM((4, *tile), f32),
            pltpu.VMEM(tile, f32),
            pltpu.VMEM(tile, f32),
            pltpu.VMEM((Z, *tile), f32),
            dma((2 * Z,)),
            dma((2 * Z,)),
        ]
    return pl.pallas_call(
        functools.partial(kernel, groups),
        out_shape=[
            jax.ShapeDtypeStruct((2, 8, width), f32),
            jax.ShapeDtypeStruct((8, width), f32),
        ],
        in_specs=[smem] * 4 + [hbm] * 2 + [vmem] * 2,
        out_specs=[vmem] * 2,
        scratch_shapes=[
            pltpu.VMEM(link_blocks.shape, f32),
            pltpu.VMEM(inverse_blocks.shape, f32),
            dma((2, link_blocks.shape[0])),
            pltpu.VMEM((4, 4, 16, width), f32),
            pltpu.VMEM((16, width), f32),
            pltpu.VMEM((K, K, 128, 128), f32),
            pltpu.VMEM((width // 2 + 16, width), f32),
            pltpu.VMEM((width, width), f32),
            pltpu.VMEM((2, 8, width), f32),
            pltpu.VMEM((2, 2, 8, width // 2), f32),
            pltpu.VMEM((2, 2, groups, 8, width // 2), f32),
            dma((len(WAVES),)),
            dma((len(WAVES),)),
            dma((len(WAVES),)),
            dma((len(WAVES),)),
            dma((8,)),
            dma((8,)),
            dma((4 * groups,)),
            dma((4 * groups,)),
            *waves,
        ],
        compiler_params=pltpu.CompilerParams(
            collective_id=0, has_side_effects=True, vmem_limit_bytes=50 << 20
        ),
        name="schur",
    )(
        block_rows, node_of, slot_count, first_diag,
        pltpu.with_memory_space_constraint(link_blocks, pltpu.HBM),
        pltpu.with_memory_space_constraint(inverse_blocks, pltpu.HBM),
        node_diag, ft,
    )


def solution(mesh):
    in_specs = (
        P(("scen", "node"), None, None),
        P(("scen", "node"), None, None),
        P(("scen", "node")),
        P(("scen", "node")),
        P(("scen", "node")),
        P("node", None),
        P("node", None, "scen"),
        P("scen"),
    )
    out_specs = (P("node", "scen", None), P("scen", None))
    return jax.shard_map(shards, mesh=mesh, in_specs=in_specs, out_specs=out_specs, check_vma=False)
```

```python
import functools

import jax
import jax.numpy as jnp
from jax import lax
from jax.experimental import pallas as pl
from jax.experimental.pallas import tpu as pltpu
from jax.sharding import PartitionSpec as P

f32, bf16 = jnp.float32, jnp.bfloat16
NN = (((1,), (0,)), ((), ()))
NT = (((1,), (1,)), ((), ()))
TN = (((0,), (0,)), ((), ()))
Z = 16
K = 4
WAVES = (
    ((0, 0),),
    ((0, 1), (0, 2), (0, 3), (1, 1)),
    ((1, 2), (1, 3), (2, 2), (2, 3), (3, 3)),
)
WAVE_OF = {block: (w, i) for w, wave in enumerate(WAVES) for i, block in enumerate(wave)}
DIRECT = 1
FAR_FIRST = (8, 7, 9, 6, 10, 5, 11, 4, 12, 3, 13, 2, 14, 1, 15)
MESH = pl.DeviceIdType.MESH


def split(x):
    high = x.astype(bf16)
    return high, (x - high.astype(f32)).astype(bf16)


def mm(a, b, dims):
    def one(p, q):
        return lax.dot_general(p, q, dims, preferred_element_type=f32)

    return one(a[0], b[0]) + (one(a[0], b[1]) + one(a[1], b[0]))


def sub_row(x, k):
    return jnp.broadcast_to(x[k : k + 1, :], (8, 128))


def lane_col(x, j):
    return jnp.broadcast_to(x[:, j : j + 1], x.shape)


def stack(parts):
    return jnp.concatenate([x[None] for x in parts], 0)


def tree(terms):
    terms = list(terms)
    while len(terms) > 1:
        terms = [
            terms[i] + terms[i + 1] if i + 1 < len(terms) else terms[i]
            for i in range(0, len(terms), 2)
        ]
    return terms[0]


def eliminate(n, hit):
    w = None
    for i in range(8):
        row = jnp.broadcast_to(n[:, i : i + 1, :], (8, 8, 128))
        p = 1.0 / row[i]
        r = lax.rsqrt(row[i])
        m = jnp.where(hit[i], 0.0, n[i])
        c = row * p
        new = jnp.where(hit[i], c, n - m * c)
        parts = [new[:i]] if i else []
        parts.append(jnp.where(hit[i], p, -m * p)[None])
        if i < 7:
            parts.append(new[i + 1 :])
        n = jnp.concatenate(parts, 0)
        mine = jnp.where(hit[i], r, 0.0)[None]
        if i:
            mine = jnp.concatenate([jnp.where(hit[i], row[:i] * r, w), mine], 0)
        w = mine
    return w, n


def diag_block(c):
    sub = lax.broadcasted_iota(jnp.int32, (8, 128), 0)
    lane = lax.broadcasted_iota(jnp.int32, (8, 128), 1)
    hit = [sub == i for i in range(8)]
    u, z = [], []
    e = stack([lane_col(c[0:8], k) for k in range(8)])
    for b in range(16):
        s, rest = 8 * b, 120 - 8 * b
        here = (lane >= s) & (lane < s + 8)
        own = c[:8]
        if rest:
            c = c[8:]
            h = [lane_col(c, s + m) for m in range(8)]
            old = [lane_col(c[:8], s + 8 + k) for k in range(8)]
        w, g = eliminate(e, hit)
        if rest:
            hn = [x[:8] for x in h]
            gc = tree(jnp.broadcast_to(g[:, j : j + 1, :], (8, 8, 128)) * hn[j] for j in range(8))
            e = stack(
                [old[k] - tree(hn[m] * sub_row(gc[m], k) for m in range(8)) for k in range(8)]
            )
        aug = jnp.where(here, jnp.where(lane == s + sub, 1.0, 0.0), own)
        rows = [sub_row(aug, k) for k in range(8)]
        u.append(
            jnp.where(lane >= s + sub, tree(w[k] * sub_row(own, k) for k in range(8)), 0.0)
        )
        z.append(jnp.where(lane < s + 8, tree(w[k] * rows[k] for k in range(8)), 0.0))
        if rest:
            scaled = tree(g[k] * rows[k] for k in range(8))
            wide = lax.broadcasted_iota(jnp.int32, (rest, 128), 1)
            c = jnp.where((wide >= s) & (wide < s + 8), 0.0, c) - tree(
                h[m] * jnp.broadcast_to(scaled[m : m + 1], (rest, 128)) for m in range(8)
            )
    return jnp.concatenate(u, 0), jnp.concatenate(z, 0)


def remote(src, dst, send, recv, to):
    return pltpu.make_async_remote_copy(
        src_ref=src, dst_ref=dst, send_sem=send, recv_sem=recv,
        device_id=to, device_id_type=MESH,
    )


def kernel(
    groups, rows, nodes, count, fd, link_hbm, inverse_hbm, diag, ft, l_out, first_out,
    link, inverse, load, f_all, f_peer, a, xt, low, l_own, g_own, got, twin_s, twin_r, swap_s, swap_r,
    f_s, f_r, end_s, end_r, *wave_refs,
):
    scen = lax.axis_index("scen")
    core, z, x = scen % 2, (scen // 2) % Z, scen // (2 * Z)
    high, kind = z // 4, z % 4
    strip = 4 * kind + high
    group = lax.axis_index("node")
    near_by = (1, 15, 2 + 12 * core)

    def chip(dz):
        return {"scen": (x * Z + (z + dz) % Z) * 2 + core}

    twin = {"scen": scen + 1 - 2 * core}
    across = {"scen": ((1 - x) * Z + z) * 2 + core}
    finals = []
    for dx in range(2):
        for c in range(2):
            for n in range(groups):
                if dx + c + n > 0:
                    to_core, to_x = (core + c) % 2, (x + dx) % 2
                    to = {"scen": (to_x * Z + z) * 2 + to_core, "node": (group + n) % groups}
                    finals.append((dx, to_core, to))
    barrier = pltpu.get_barrier_semaphore()
    greet = [chip(d) for d in range(1, Z)] + [to for *_, to in finals]
    for to in greet:
        pl.semaphore_signal(barrier, inc=1, device_id=to, device_id_type=MESH)

    slots = link.shape[0]
    for i in range(slots):
        for n, (src, dst) in enumerate(((link_hbm, link), (inverse_hbm, inverse))):
            pltpu.make_async_copy(src.at[i], dst.at[i], load.at[n, i]).start()

    per = len(wave_refs) // len(WAVES)
    waves = [wave_refs[per * w : per * w + per] for w in range(len(WAVES))]
    sent = []

    def go(src, dst, send, recv, to):
        copy = remote(src, dst, send, recv, to)
        copy.start()
        sent.append(copy)
        return copy

    def arrive(copies):
        for copy in copies:
            copy.wait_recv()

    for acc, *_ in waves:
        acc[...] = jnp.zeros_like(acc)
    row_id = lax.broadcasted_iota(jnp.int32, (link.shape[1], 1), 0)

    def slot(i, carry):
        pltpu.make_async_copy(link_hbm.at[i], link.at[i], load.at[0, i]).wait()
        pltpu.make_async_copy(inverse_hbm.at[i], inverse.at[i], load.at[1, i]).wait()
        limit = jnp.where(i < count[0], rows[i], 0)
        masked = jnp.where(row_id < limit, link[i], 0.0)
        first = nodes[i] == 2 * group
        m = split(masked)
        y = split(mm(split(inverse[i]), m, NN))
        for q in range(K):
            lo = 128 * q
            term = mm(
                (m[0][:, lo : lo + 128], m[1][:, lo : lo + 128]),
                (y[0][:, lo:], y[1][:, lo:]),
                TN,
            )
            for j in range(K - q):
                w, p = WAVE_OF[q, q + j]
                acc = waves[w][0]
                part = term[:, 128 * j : 128 * j + 128].reshape(16, 8, 128)
                acc[0, :, p] += jnp.where(first, part, 0.0)
                acc[1, :, p] += jnp.where(first, 0.0, part)
        return carry

    lax.fori_loop(0, slots, slot, 0)
    pl.semaphore_wait(barrier, len(greet))

    twins = []
    for w, (acc, sib, *_) in enumerate(waves):
        twins.append(go(acc.at[1 - core], sib, twin_s.at[w], twin_r.at[w], twin))
        if w == 0:
            f_own = f_all.at[high, kind, pl.ds(core * 8, 8), :]
            f_twin = go(ft.at[1 - core], f_own, f_s.at[0], f_r.at[0], twin)
    f_all[high, kind, pl.ds(core * 8, 8), :] = ft[core]

    if DIRECT:
        acc, sib, rs, _, mine0, peer0, s0, s_sem, r_sem = waves[0]
        twins[0].wait_recv()
        acc[core] += sib[...]
        direct = []
        for d in FAR_FIRST:
            to = (z + d) % Z
            direct.append(
                go(acc.at[core, 4 * (to % 4) + to // 4], rs.at[z], s_sem.at[d], r_sem.at[d], chip(d))
            )
        rs[z] = acc[core, strip]
    f_twin.wait_recv()
    f_across = go(f_all.at[high, kind], f_peer, f_s.at[1], f_r.at[1], across)
    near = {}
    for w in range(DIRECT, len(WAVES)):
        acc, sib, rs, half, mine, peer, s_all, s_sem, r_sem = waves[w]
        twins[w].wait_recv()
        acc[core] += sib[...]
        near[w] = [
            go(
                acc.at[core, pl.ds(4 * ((z + d) % 4), 4)], rs.at[pl.ds(4 * i, 4)],
                s_sem.at[i], r_sem.at[i], chip(d),
            )
            for i, d in enumerate(near_by)
        ]
    far = {}
    for w in range(DIRECT, len(WAVES)):
        acc, sib, rs, half, mine, peer, s_all, s_sem, r_sem = waves[w]
        arrive(near[w])
        half[...] = (acc[core, pl.ds(4 * kind, 4)] + rs[0:4]) + (rs[4:8] + rs[8:12])
        far[w] = [
            go(half.at[(high + k) % 4], rs.at[11 + k], s_sem.at[2 + k], r_sem.at[2 + k], chip(4 * k))
            for k in (2, 1, 3)
        ]

    piece = f_all.at[high, kind]
    f_far = [go(piece, piece, f_s.at[1 + k], f_r.at[1 + k], chip(4 * k)) for k in (2, 1, 3)]

    def swap(w):
        acc, sib, rs, half, mine, peer, *_ = waves[w]
        if w < DIRECT:
            arrive(direct)
            mine[...] = tree(rs[i] for i in range(Z))
        else:
            arrive(far[w])
            mine[...] = (half[high] + rs[12]) + (rs[13] + rs[14])
        return go(mine, peer, swap_s.at[w], swap_r.at[w], across)

    sub = lax.broadcasted_iota(jnp.int32, (8, 128), 0)
    lane = lax.broadcasted_iota(jnp.int32, (8, 128), 1)

    def spread(w, swapped):
        acc, sib, rs, half, mine, peer, s_all, s_sem, r_sem = waves[w]
        swapped.wait_recv()
        s_all[strip] = mine[...] + peer[...]
        for q in range(K):
            if WAVE_OF[q, q][0] == w:
                d = diag[:, 128 * q : 128 * q + 128]
                d = jnp.broadcast_to(jnp.where(core == 0, d[0:1], d[1:2]), (8, 128))
                s_all[strip, WAVE_OF[q, q][1]] += jnp.where(lane == 8 * strip + sub, d, 0.0)
        own = s_all.at[strip]
        if w < DIRECT:
            return [
                go(own, own, s_sem.at[16 + d], r_sem.at[16 + d], chip(d)) for d in FAR_FIRST
            ]
        return [
            go(own, own, s_sem.at[5 + k], r_sem.at[5 + k], chip(4 * k)) for k in (2, 1, 3)
        ]

    def pass_on(w, copies):
        s_all, s_sem, r_sem = waves[w][6:]
        arrive(copies)
        piece = s_all.at[pl.ds(4 * kind, 4)]
        return [
            go(piece, piece, s_sem.at[9 + i], r_sem.at[9 + i], chip(d))
            for i, d in enumerate(near_by)
        ]

    gathers = {}
    if DIRECT:
        gathers[0] = spread(0, swap(0))
    swaps = {}
    for w in range(DIRECT, len(WAVES)):
        swaps[w] = swap(w)
        if w - 1 in swaps:
            gathers[w - 1] = spread(w - 1, swaps[w - 1])
    gathers[w] = spread(w, swaps[w])

    def block(i, j):
        w, p = WAVE_OF[i, j]
        return waves[w][6][:, p].reshape(128, 128)

    low[...] = jnp.zeros_like(low)
    us, invs = {}, []
    own_half = xt.shape[0] - 16

    def columns(lo):
        half = f_all[...].reshape(own_half, -1)[:, lo : lo + 128]
        return jnp.concatenate([half, f_peer[:, lo : lo + 128]], 0)

    def solve(q):
        lo = 128 * q
        xq = mm(split(columns(lo) if q == 0 else xt[:, lo : lo + 128]), invs[q], NT)
        xs = split(xq)
        for j in range(q + 1, K):
            hi = 128 * j
            old = columns(hi) if q == 0 else xt[:, hi : hi + 128]
            xt[:, hi : hi + 128] = old - mm(xs, us[q, j], NN)
        xt[:, lo : lo + 128] = xq

    done = set()

    def ready(row):
        for j in range(row, K):
            w = WAVE_OF[row, j][0]
            if w not in done:
                done.add(w)
                arrive(gathers[w])

    if not DIRECT:
        gathers[0] = pass_on(0, gathers[0])
    arrive(gathers[0])
    done.add(0)
    for q in range(K):
        lo = 128 * q
        u, inv = diag_block(block(0, 0) if q == 0 else a[q, q])
        low[lo : lo + 128, lo : lo + 128] = u.T
        invs.append(split(inv))
        if q == 0:
            for w in range(1, len(WAVES)):
                gathers[w] = pass_on(w, gathers[w])
            arrive(f_far)
            piece = f_all.at[:, kind]
            f_near = [
                go(piece, piece, f_s.at[5 + i], f_r.at[5 + i], chip(d))
                for i, d in enumerate(near_by)
            ]
            ready(0)
        for j in range(q + 1, K):
            v = mm(invs[q], split(block(0, j) if q == 0 else a[q, j]), NN)
            low[128 * j : 128 * j + 128, lo : lo + 128] = v.T
            us[q, j] = split(v)
        if q == 0:
            ready(1)
            for j in range(1, K):
                a[1, j] = block(1, j) - mm(us[0, 1], us[0, j], TN)
        elif q == 1:
            ready(2)
            ready(3)
            for i in range(2, K):
                for j in range(i, K):
                    a[i, j] = block(i, j) - (
                        mm(us[0, i], us[0, j], TN) + mm(us[1, i], us[1, j], TN)
                    )
        elif q == 2:
            a[3, 3] -= mm(us[2, 3], us[2, 3], TN)
            arrive(f_near + [f_across])
            for p in range(3):
                solve(p)
        else:
            solve(3)

    own = pl.multiple_of((x * Z + z) * 16, 16)
    width = first_out.shape[1]
    l_own[0] = low[pl.ds(own, 8), :]
    l_own[1] = low[pl.ds(pl.multiple_of(own + 8, 8), 8), :]
    factor = go(l_own.at[1 - core], l_out.at[core], end_s.at[0], end_r.at[0], twin)
    l_out[core] = l_own[core]
    wanted = jnp.concatenate([xt[pl.ds(pl.multiple_of(16 * z, 16), 16), :], xt[own_half:, :]], 0)
    term = mm(split(wanted), split(xt[:own_half, :]), NT)
    for dx in range(2):
        for c in range(2):
            lo = 16 * dx + 8 * c
            g_own[dx, c] = term[lo : lo + 8]
    last = [
        go(g_own.at[dx, to_core], got.at[x, core, group], end_s.at[1 + i], end_r.at[1 + i], to)
        for i, (dx, to_core, to) in enumerate(finals)
    ]
    got[x, core, group] = g_own[0, core]
    arrive(last)
    row8 = lax.broadcasted_iota(jnp.int32, (8, width), 0)
    col8 = lax.broadcasted_iota(jnp.int32, (8, width), 1)
    d = jnp.zeros((8, width), f32)
    for i in range(8):
        d = jnp.where(row8 == i, fd[i], d)
    total = jnp.concatenate(
        [tree(got[h, c, n] for c in range(2) for n in range(groups)) for h in range(2)], 1
    )
    first_out[...] = total + jnp.where(col8 == scen * 8 + row8, d, 0.0)
    factor.wait_recv()
    for copy in sent:
        copy.wait_send()


def shards(
    link_blocks, inverse_blocks, block_rows, node_of, slot_count, node_diag, first_link, first_diag
):
    groups = lax.axis_size("node")
    width = link_blocks.shape[2]
    ft = jnp.swapaxes(first_link, 1, 2)
    vmem = pl.BlockSpec(memory_space=pltpu.VMEM)
    smem = pl.BlockSpec(memory_space=pltpu.SMEM)
    hbm = pl.BlockSpec(memory_space=pltpu.HBM)
    dma = pltpu.SemaphoreType.DMA
    waves = []
    for wave in WAVES:
        tile = (len(wave), 8, 128)
        waves += [
            pltpu.VMEM((2, Z, *tile), f32),
            pltpu.VMEM((Z, *tile), f32),
            pltpu.VMEM((Z, *tile), f32),
            pltpu.VMEM((4, *tile), f32),
            pltpu.VMEM(tile, f32),
            pltpu.VMEM(tile, f32),
            pltpu.VMEM((Z, *tile), f32),
            dma((2 * Z,)),
            dma((2 * Z,)),
        ]
    return pl.pallas_call(
        functools.partial(kernel, groups),
        out_shape=[
            jax.ShapeDtypeStruct((2, 8, width), f32),
            jax.ShapeDtypeStruct((8, width), f32),
        ],
        in_specs=[smem] * 4 + [hbm] * 2 + [vmem] * 2,
        out_specs=[vmem] * 2,
        scratch_shapes=[
            pltpu.VMEM(link_blocks.shape, f32),
            pltpu.VMEM(inverse_blocks.shape, f32),
            dma((2, link_blocks.shape[0])),
            pltpu.VMEM((4, 4, 16, width), f32),
            pltpu.VMEM((16, width), f32),
            pltpu.VMEM((K, K, 128, 128), f32),
            pltpu.VMEM((width // 2 + 16, width), f32),
            pltpu.VMEM((width, width), f32),
            pltpu.VMEM((2, 8, width), f32),
            pltpu.VMEM((2, 2, 8, width // 2), f32),
            pltpu.VMEM((2, 2, groups, 8, width // 2), f32),
            dma((len(WAVES),)),
            dma((len(WAVES),)),
            dma((len(WAVES),)),
            dma((len(WAVES),)),
            dma((8,)),
            dma((8,)),
            dma((4 * groups,)),
            dma((4 * groups,)),
            *waves,
        ],
        compiler_params=pltpu.CompilerParams(
            collective_id=0, has_side_effects=True, vmem_limit_bytes=50 << 20
        ),
        name="schur",
    )(
        block_rows, node_of, slot_count, first_diag,
        pltpu.with_memory_space_constraint(link_blocks, pltpu.HBM),
        pltpu.with_memory_space_constraint(inverse_blocks, pltpu.HBM),
        node_diag, ft,
    )


def solution(mesh):
    in_specs = (
        P(("scen", "node"), None, None),
        P(("scen", "node"), None, None),
        P(("scen", "node")),
        P(("scen", "node")),
        P(("scen", "node")),
        P("node", None),
        P("node", None, "scen"),
        P("scen"),
    )
    out_specs = (P("node", "scen", None), P("scen", None))
    return jax.shard_map(shards, mesh=mesh, in_specs=in_specs, out_specs=out_specs, check_vma=False)
```
